32 devices in a mesh: groups: 2 (over x), row: 2 (over core), col: 8 (over z, y).
Axes of the slice: x: 2, y: 2, z: 4, core: 2. Of those that a mesh axis runs over, the one named last changes fastest.
Arguments:
- pair: bfloat16 [1280, 640, 128], P(('groups', 'col'), 'row'), parts along dimension 0, may hold values from -6 to 6
- token_mask: int32 [1280], P('groups'), parts along dimension 0, may hold values 0 or 1
- start_gain: float32 [128], replicated, may hold values from 0.25 to 1.75
- start_head_gain: float32 [128], replicated, may hold values from 0.25 to 1.75
- start_in: bfloat16 [128, 512], replicated, may hold values from -0.5 to 0.5
- start_out: bfloat16 [128, 128], replicated, may hold values from -0.5 to 0.5
- end_gain: float32 [128], replicated, may hold values from 0.25 to 1.75
- end_head_gain: float32 [128], replicated, may hold values from 0.25 to 1.75
- end_in: bfloat16 [128, 512], replicated, may hold values from -0.5 to 0.5
- end_out: bfloat16 [128, 128], replicated, may hold values from -0.5 to 0.5
- trans_gain: float32 [128], replicated, may hold values from 0.25 to 1.75
- trans_in: bfloat16 [128, 1024], replicated, may hold values from -0.5 to 0.5
- trans_out: bfloat16 [512, 128], replicated, may hold values from -0.25 to 0.25
Outputs:
- update_start: bfloat16 [1280, 640, 128], P(('groups', 'col'), 'row'), parts along dimension 0
- update_end: bfloat16 [1280, 640, 128], P(('groups', 'col'), 'row'), parts along dimension 0
- update_trans: bfloat16 [1280, 640, 128], P(('groups', 'col'), 'row'), parts along dimension 0
The draws below stay inside these ranges and needn't reach their ends.
There are 2 independent parts, one for each index of `groups`. The reference program is written for one: setup_inputs(seed, part) draws one part's arguments, and reference() takes and returns one part's arrays. A program takes and returns all parts, laid end to end along the dimension named above; an argument that names none is the same for every part. Nothing has to cross between parts.
Inputs may be any that keep to these rules, and one draw needn't show every extreme that they name: `token_mask`: 1 marks a valid token of the complex, 0 a padded one.
All inputs are finite; a program needn't handle non-finite values.
Results may differ from the reference program's by a relative error of at most 0.018.
Values may be sent and summed in bfloat16 or wider, within the bound.
No kernel may reach another device: no remote copies, remote signals or barrier semaphores. Data moves between devices by JAX's collectives and lax.ppermute only.
A program may use at most 192 MiB of HBM per device.

```python
import jax
import jax.numpy as jnp
from jax import lax

N = 640
C = 128
HEADS = 4
TRANS = 512
N_ROW = 2
N_COL = 8


def touch_ends(result, key, low, high):
    longest = result.shape.index(max(result.shape))
    spots = []
    for shift in (0, 1):
        where = [jax.random.randint(jax.random.fold_in(key, axis), (), 0, length) for axis, length in enumerate(result.shape)]
        where[longest] = (where[longest] + shift) % result.shape[longest]
        spots.append(tuple(where))
    return result.at[spots[0]].set(low).at[spots[1]].set(high)


def block_levels(key, shape, split, least, top_value):
    def one(position, parts):
        draws = jax.random.uniform(jax.random.fold_in(jax.random.fold_in(key, 6), position), (parts,), jnp.float32, least / len(split), top_value / len(split))
        return jnp.repeat(jnp.exp(draws), shape[position] // parts).reshape((-1,) + (1,) * (len(shape) - position - 1))

    loudness = one(*split[0])
    for cut in split[1:]:
        loudness = loudness * one(*cut)
    return loudness


def normal_values(own_key, dims, deviation, limit, split=(), dtype=jnp.bfloat16):
    values = jax.random.normal(own_key, dims, jnp.float32) * deviation
    if len(split) > 0:
        values = block_levels(own_key, dims, split, -0.22, 0.18) * values
    return jnp.clip(values, min=-limit, max=limit).astype(dtype)


def setup_inputs(seed: int = 0, part: int = 0) -> dict:
    splits = jax.random.split(jax.random.key(seed), 14)
    own_keys = jax.random.split(jax.random.fold_in(splits[13], part), 14)
    return {
        "pair": normal_values(own_keys[0], (N, N, C), 1.0, 6.0, ((0, 8), (1, 2))),
        "token_mask": touch_ends((jax.random.randint(own_keys[1], (N,), 0, 8) < 7).astype(jnp.int32), jax.random.fold_in(own_keys[1], 1), 0, 1),
        "start_gain": jnp.clip(1.0 + 0.15 * jax.random.normal(splits[2], (C,), jnp.float32), 0.25, 1.75),
        "start_head_gain": jnp.clip(1.0 + 0.15 * jax.random.normal(splits[3], (C,), jnp.float32), 0.25, 1.75),
        "start_in": normal_values(splits[4], (C, 4 * C), C ** -0.5, 0.5),
        "start_out": normal_values(splits[5], (C, C), C ** -0.5, 0.5),
        "end_gain": jnp.clip(1.0 + 0.15 * jax.random.normal(splits[6], (C,), jnp.float32), 0.25, 1.75),
        "end_head_gain": jnp.clip(1.0 + 0.15 * jax.random.normal(splits[7], (C,), jnp.float32), 0.25, 1.75),
        "end_in": normal_values(splits[8], (C, 4 * C), C ** -0.5, 0.5),
        "end_out": normal_values(splits[9], (C, C), C ** -0.5, 0.5),
        "trans_gain": jnp.clip(1.0 + 0.15 * jax.random.normal(splits[10], (C,), jnp.float32), 0.25, 1.75),
        "trans_in": normal_values(splits[11], (C, 2 * TRANS), C ** -0.5, 0.5),
        "trans_out": normal_values(splits[12], (TRANS, C), TRANS ** -0.5, 0.25),
    }


EPSILON = 1e-05

def layer_norm(values, scales):
    average = lax.optimization_barrier(jnp.mean(values, axis=-1, keepdims=True))
    centered = values - average
    variance = lax.optimization_barrier(jnp.mean(centered * centered, axis=-1, keepdims=True))
    return centered * lax.rsqrt(variance + EPSILON) * scales.astype(jnp.float32)

def feature(values):
    return jax.nn.elu(values) + 1.0

def triangle(field, valid, ln_gain, head_gain, w_in, w_out, blocks):
    row_count, col_count, width = field.shape
    depth = width // HEADS
    stride = 16

    def one_block(operands):
        block, row_valid = operands
        normed = layer_norm(block, ln_gain).astype(jnp.bfloat16)
        project = jnp.dot(normed.reshape(-1, width), w_in, preferred_element_type=jnp.float32)
        project = project.reshape(stride, col_count, 4 * width)
        pair_valid = row_valid[:, None] * valid[None, :]
        queries = feature(project[..., :width]).astype(jnp.bfloat16).reshape(stride, col_count, HEADS, depth)
        key_feat = (feature(project[..., width:2 * width]) * pair_valid[..., None]).astype(jnp.bfloat16)
        key_feat = key_feat.reshape(stride, blocks, col_count // blocks, HEADS, depth)
        values = project[..., 2 * width:3 * width].astype(jnp.bfloat16)
        values = values.reshape(stride, blocks, col_count // blocks, HEADS, depth)
        gating = jax.nn.sigmoid(project[..., 3 * width:])
        partial_value = jnp.einsum('rbkhd,rbkhe->rbhde', key_feat.astype(jnp.float32), values.astype(jnp.float32))
        state = lax.optimization_barrier(jnp.sum(lax.optimization_barrier(partial_value.astype(jnp.bfloat16)).astype(jnp.float32), axis=1))
        key_part = lax.optimization_barrier(jnp.sum(key_feat.astype(jnp.float32), axis=2))
        totals = lax.optimization_barrier(jnp.sum(lax.optimization_barrier(key_part.astype(jnp.bfloat16)).astype(jnp.float32), axis=1))
        query_f = queries.astype(jnp.float32)
        numer = jnp.einsum('rkhd,rhde->rkhe', query_f, state)
        denom = jnp.maximum(jnp.einsum('rkhd,rhd->rkh', query_f, totals), 1.0)
        attended = (numer / denom[..., None]).reshape(stride, col_count, width)
        scaled = attended * lax.rsqrt(lax.optimization_barrier(jnp.mean(attended * attended, axis=-1, keepdims=True)) + EPSILON)
        scaled = (scaled * head_gain.astype(jnp.float32) * gating).astype(jnp.bfloat16)
        update = jnp.dot(scaled.reshape(-1, width), w_out, preferred_element_type=jnp.float32)
        return update.astype(jnp.bfloat16).reshape(stride, col_count, width)
    pieces = lax.map(one_block, (field.reshape(row_count // stride, stride, col_count, width), valid.reshape(row_count // stride, stride)))
    return pieces.reshape(row_count, col_count, width)

def reference(pair, token_mask, start_gain, start_head_gain, start_in, start_out, end_gain, end_head_gain, end_in, end_out, trans_gain, trans_in, trans_out):
    valid = token_mask.astype(jnp.float32)
    anchor = pair.astype(jnp.float32)
    update_start = triangle(anchor, valid, start_gain, start_head_gain, start_in, start_out, N_ROW)
    first_sum = anchor + update_start.astype(jnp.float32)
    flipped = triangle(jnp.transpose(first_sum, (1, 0, 2)), valid, end_gain, end_head_gain, end_in, end_out, N_COL)
    update_end = jnp.transpose(flipped, (1, 0, 2))
    second_sum = first_sum + update_end.astype(jnp.float32)
    width = pair.shape[2]
    hidden_width = trans_out.shape[0]
    stride = 16

    def transition(block):
        normed = layer_norm(block, trans_gain).astype(jnp.bfloat16)
        lifted = jnp.dot(normed.reshape(-1, width), trans_in, preferred_element_type=jnp.float32)
        hidden = (jax.nn.silu(lifted[:, :hidden_width]) * lifted[:, hidden_width:]).astype(jnp.bfloat16)
        return jnp.dot(hidden, trans_out, preferred_element_type=jnp.float32).astype(jnp.bfloat16)
    row_count = pair.shape[0]
    update_trans = lax.map(transition, second_sum.reshape(row_count // stride, stride, row_count, width))
    update_trans = update_trans.reshape(row_count, row_count, width)
    return (update_start, update_end, update_trans)
```

```python
import functools
import math

import jax
import jax.numpy as jnp
from jax import lax
from jax.experimental import pallas as pl
from jax.experimental.pallas import tpu as pltpu
from jax.sharding import PartitionSpec as P

HEADS = 4
EPSILON = 1e-05
CHUNKS = 2
BF16 = jnp.bfloat16
F32 = jnp.float32
NT = (((1,), (1,)), ((), ()))


def params():
    return pltpu.CompilerParams(
        dimension_semantics=("arbitrary",), vmem_limit_bytes=56 * 1024 * 1024
    )


def norm(values, gain):
    inverse = 1.0 / values.shape[-1]
    centered = values - jnp.sum(values, axis=-1, keepdims=True) * inverse
    variance = jnp.sum(centered * centered, axis=-1, keepdims=True) * inverse
    return (centered * lax.rsqrt(variance + EPSILON) * gain).astype(BF16)


def feature(values):
    return jnp.where(values > 0, values + 1.0, jnp.exp(values))


def key_state(keys, values, mask_row):
    width = keys.shape[-1]
    depth = width // HEADS
    turned = values.T * mask_row
    ones = jnp.broadcast_to(mask_row, (16, mask_row.shape[-1]))
    full = jnp.dot(jnp.concatenate([turned, ones], axis=0), keys, preferred_element_type=F32)
    lane_head = lax.broadcasted_iota(jnp.int32, (depth, width), 1) // depth
    packed = jnp.zeros((depth, width), F32)
    for head in range(HEADS):
        packed = jnp.where(lane_head == head, full[head * depth : (head + 1) * depth], packed)
    return packed, full[width : width + 1]


def attend(queries, packed, totals, block_mask):
    width = queries.shape[-1]
    depth = width // HEADS
    spread = jnp.concatenate([packed] * HEADS, axis=0)
    right = jnp.concatenate([spread, jnp.broadcast_to(totals, (width, width))], axis=0)
    both = lax.dot_general(queries, right * block_mask, NT, preferred_element_type=F32)
    return both[:, :width] / jnp.maximum(both[:, width:], 1.0)


def head_norm(attended, gain, gate):
    inverse = 1.0 / attended.shape[-1]
    square = jnp.sum(attended * attended, axis=-1, keepdims=True) * inverse
    return attended * lax.rsqrt(square + EPSILON) * gain * gate


def start_kernel(row_mask, pair, col_mask, gain, w_in, query_out, gate_out, state_out, total_out):
    rows, cols, width = pair.shape
    base = pl.program_id(0) * rows
    w = w_in[...]
    for r in range(rows):
        x = norm(pair[r].astype(F32), gain[...])
        project = jnp.dot(x, w, preferred_element_type=F32)
        query_out[r] = feature(project[:, :width]).astype(BF16)
        keys = feature(project[:, width : 2 * width]).astype(BF16)
        values = project[:, 2 * width : 3 * width].astype(BF16)
        gate_out[r] = (jnp.tanh(project[:, 3 * width :]) + 1.0).astype(BF16)
        packed, totals = key_state(keys, values, col_mask[...])
        valid = row_mask[base + r].astype(F32)
        state_out[r] = (packed * valid).astype(BF16)
        total_out[r] = (totals * valid).astype(BF16)


def middle_kernel(
    steps,
    col_mask,
    pair,
    query,
    gate,
    state_a,
    state_b,
    total_a,
    total_b,
    block_mask,
    row_mask,
    head_gain,
    w_out,
    gain,
    w_in,
    *rest,
):
    update_out, query_out, gate_out, state_out, total_out, anchor = rest[-6:]
    block_rows, cols, width = pair.shape
    rows = query_out.shape[1]
    block_cols = query_out.shape[0]
    step = pl.program_id(0)

    @pl.when(step < steps)
    def _():
        for r in range(block_rows):
            packed = (state_a[r].astype(F32) + state_b[r].astype(F32)).astype(BF16)
            totals = (total_a[r].astype(F32) + total_b[r].astype(F32)).astype(BF16)
            attended = attend(query[r], packed, totals, block_mask[...])
            scaled = head_norm(attended, head_gain[...], gate[r].astype(F32)).astype(BF16)
            update = jnp.dot(scaled, w_out[...], preferred_element_type=F32).astype(BF16)
            update_out[r] = update
            first = pair[r].astype(F32) + update.astype(F32)
            anchor[pl.ds((step * block_rows + r) * cols, cols), :] = first

    @pl.when(step >= steps)
    def _():
        base = (step - steps) * block_cols
        w = w_in[...]
        for c in range(block_cols):
            x = norm(anchor[pl.ds(base + c, rows, stride=cols), :], gain[...])
            project = jnp.dot(x, w, preferred_element_type=F32)
            query_out[c] = feature(project[:, :width]).astype(BF16)
            keys = feature(project[:, width : 2 * width]).astype(BF16)
            values = project[:, 2 * width : 3 * width].astype(BF16)
            gate_out[c] = (jnp.tanh(project[:, 3 * width :]) + 1.0).astype(BF16)
            packed, totals = key_state(keys, values, row_mask[...])
            valid = col_mask[base + c].astype(F32)
            state_out[c] = (packed * valid).astype(BF16)
            total_out[c] = (totals * valid).astype(BF16)


def end_kernel(
    pair,
    update_start,
    query,
    gate,
    state,
    total,
    block_mask,
    head_gain,
    w_out,
    gain,
    w_in,
    w_down,
    *rest,
):
    update_out, trans_out, turned = rest[-3:]
    rows, block_cols, width = pair.shape
    hidden = w_down.shape[0]
    for c in range(block_cols):
        attended = attend(query[c], state[c], total[c], block_mask[...])
        scaled = head_norm(attended, head_gain[...], gate[c].astype(F32)).astype(BF16)
        update = jnp.dot(scaled, w_out[...], preferred_element_type=F32)
        turned[pl.ds(c, rows, stride=block_cols), :] = update
    slab = math.gcd(rows, 8)
    for r in range(0, rows, slab):
        update = turned[pl.ds(r * block_cols, slab * block_cols), :].astype(BF16)
        update_out[pl.ds(r, slab)] = update.reshape(slab, block_cols, width)
        first = pair[pl.ds(r, slab)].astype(F32) + update_start[pl.ds(r, slab)].astype(F32)
        second = first.reshape(slab * block_cols, width) + update.astype(F32)
        x = norm(second, gain[...])
        lifted = jnp.dot(x, w_in[...], preferred_element_type=F32)
        half = lifted[:, :hidden]
        inner = (half * (1.0 + jnp.tanh(half)) * lifted[:, hidden:]).astype(BF16)
        down = jnp.dot(inner, w_down[...], preferred_element_type=F32)
        trans_out[pl.ds(r, slab)] = down.reshape(slab, block_cols, width).astype(BF16)


def whole(shape):
    return pl.BlockSpec(shape, lambda *_: (0,) * len(shape), pipeline_mode=pl.Buffered(1))


def shards(
    pair,
    token_mask,
    start_gain,
    start_head_gain,
    start_in,
    start_out,
    end_gain,
    end_head_gain,
    end_in,
    end_out,
    trans_gain,
    trans_in,
    trans_out,
):
    rows, cols, width = pair.shape
    depth = width // HEADS
    hidden = trans_out.shape[0]
    row_ids = lax.dynamic_slice_in_dim(token_mask, lax.axis_index("col") * rows, rows)
    col_ids = lax.dynamic_slice_in_dim(token_mask, lax.axis_index("row") * cols, cols)
    row_line = row_ids.astype(BF16)[None, :]
    col_line = col_ids.astype(BF16)[None, :]
    lanes = jnp.arange(width) // depth
    block_mask = jnp.tile((lanes[:, None] == lanes[None, :]).astype(BF16), (2, 1))
    halve = jnp.where(jnp.arange(4 * width) < 3 * width, 1.0, 0.5).astype(BF16)
    start_w = start_in * halve
    end_w = end_in * halve
    lift_w = trans_in * jnp.where(jnp.arange(2 * hidden) < hidden, 0.5, 1.0).astype(BF16)
    line = lambda gain: gain[None, :]

    tall = math.gcd(rows, 4)
    shape = jax.ShapeDtypeStruct
    block = lambda *dims: pl.BlockSpec(dims, lambda n, *_: (n,) + (0,) * (len(dims) - 1))
    query, gate, state, total = pl.pallas_call(
        start_kernel,
        grid_spec=pltpu.PrefetchScalarGridSpec(
            num_scalar_prefetch=1,
            grid=(rows // tall,),
            in_specs=[
                block(tall, cols, width),
                whole((1, cols)),
                whole((1, width)),
                whole((width, 4 * width)),
            ],
            out_specs=[
                block(tall, cols, width),
                block(tall, cols, width),
                block(tall, depth, width),
                block(tall, 1, width),
            ],
        ),
        out_shape=[
            shape((rows, cols, width), BF16),
            shape((rows, cols, width), BF16),
            shape((rows, depth, width), BF16),
            shape((rows, 1, width), BF16),
        ],
        compiler_params=params(),
        name="start",
    )(row_ids, pair, col_line, line(start_gain), start_w)

    swap = [(n, lax.axis_size("row") - 1 - n) for n in range(lax.axis_size("row"))]
    state_b = lax.ppermute(state, "row", swap)
    total_b = lax.ppermute(total, "row", swap)

    chunk = cols // CHUNKS
    wide = 16
    steps = rows // tall
    turns = chunk // wide

    def middle(part, update):
        low = lambda n: jnp.minimum(n, steps - 1)
        high = lambda n: jnp.maximum(n - steps, 0)
        tile = pl.BlockSpec((tall, chunk, width), lambda n, *_: (low(n), part, 0))
        by_row = lambda *dims: pl.BlockSpec(dims, lambda n, *_: (low(n), 0, 0))
        by_col = lambda *dims: pl.BlockSpec(dims, lambda n, *_: (high(n), 0, 0))
        extra = [] if update is None else [update]
        return pl.pallas_call(
            functools.partial(middle_kernel, steps),
            grid_spec=pltpu.PrefetchScalarGridSpec(
                num_scalar_prefetch=1,
                grid=(steps + turns,),
                in_specs=[
                    tile,
                    tile,
                    tile,
                    by_row(tall, depth, width),
                    by_row(tall, depth, width),
                    by_row(tall, 1, width),
                    by_row(tall, 1, width),
                    whole((2 * width, width)),
                    whole((1, rows)),
                    whole((1, width)),
                    whole((width, width)),
                    whole((1, width)),
                    whole((width, 4 * width)),
                ]
                + [pl.BlockSpec(memory_space=pl.ANY)] * len(extra),
                out_specs=[
                    tile,
                    by_col(wide, rows, width),
                    by_col(wide, rows, width),
                    by_col(wide, depth, width),
                    by_col(wide, 1, width),
                ],
                scratch_shapes=[pltpu.VMEM((rows * chunk, width), F32)],
            ),
            out_shape=[
                shape((rows, cols, width), BF16),
                shape((chunk, rows, width), BF16),
                shape((chunk, rows, width), BF16),
                shape((chunk, depth, width), BF16),
                shape((chunk, 1, width), BF16),
            ],
            input_output_aliases={14: 0} if extra else {},
            compiler_params=params(),
            name="middle",
        )(
            lax.slice_in_dim(col_ids, part * chunk, (part + 1) * chunk),
            pair,
            query,
            gate,
            state,
            state_b,
            total,
            total_b,
            block_mask,
            row_line,
            line(start_head_gain * 0.5),
            start_out,
            line(end_gain),
            end_w,
            *extra,
        )

    def end(part, update_start, parts, outs):
        offset = part * turns
        tile = pl.BlockSpec((rows, wide, width), lambda n: (0, offset + n, 0))
        return pl.pallas_call(
            end_kernel,
            grid=(turns,),
            in_specs=[
                tile,
                tile,
                block(wide, rows, width),
                block(wide, rows, width),
                block(wide, depth, width),
                block(wide, 1, width),
                whole((2 * width, width)),
                whole((1, width)),
                whole((width, width)),
                whole((1, width)),
                whole((width, 2 * hidden)),
                whole((hidden, width)),
            ]
            + [pl.BlockSpec(memory_space=pl.ANY)] * len(outs),
            out_specs=[tile, tile],
            scratch_shapes=[pltpu.VMEM((rows * wide, width), F32)],
            out_shape=[shape((rows, cols, width), BF16)] * 2,
            input_output_aliases={12: 0, 13: 1} if outs else {},
            compiler_params=params(),
            name="end",
        )(
            pair,
            update_start,
            *parts,
            block_mask,
            line(end_head_gain * 0.5),
            end_out,
            line(trans_gain),
            lift_w,
            trans_out,
            *outs,
        )

    update_start = None
    held = []
    for part in range(CHUNKS):
        update_start, query_e, gate_e, state_e, total_e = middle(part, update_start)
        state_e = lax.psum(state_e, "col")
        total_e = lax.psum(total_e, "col")
        held.append((query_e, gate_e, state_e, total_e))
    outs = ()
    for part in range(CHUNKS):
        outs = end(part, update_start, held[part], outs)
    return (update_start, outs[0], outs[1])


def solution(mesh):
    pair_spec = P(("groups", "col"), "row", None)
    return jax.shard_map(
        shards,
        mesh=mesh,
        in_specs=(pair_spec, P("groups")) + (P(),) * 11,
        out_specs=(pair_spec,) * 3,
        check_vma=False,
    )
```

```python
import functools
import math

import jax
import jax.numpy as jnp
from jax import lax
from jax.experimental import pallas as pl
from jax.experimental.pallas import tpu as pltpu
from jax.sharding import PartitionSpec as P

HEADS = 4
EPSILON = 1e-05
CHUNKS = 4
BF16 = jnp.bfloat16
F32 = jnp.float32
NT = (((1,), (1,)), ((), ()))


def params():
    return pltpu.CompilerParams(
        dimension_semantics=("arbitrary",),
        vmem_limit_bytes=56 * 1024 * 1024,
    )


def cost(pairs, products):
    return pl.CostEstimate(
        flops=16 * pairs * products, transcendentals=0, bytes_accessed=64 * pairs
    )


def norm(values, gain):
    width = values.shape[-1]
    centered = values - jnp.sum(values, axis=-1, keepdims=True) * (1.0 / width)
    square = jnp.sum(centered * centered, axis=-1, keepdims=True)
    return (centered * lax.rsqrt(square + EPSILON * width) * (gain * math.sqrt(width))).astype(BF16)


def feature(values):
    values = values.astype(BF16)
    return jnp.where(values > 0, values + 1.0, jnp.exp(values))


def gating(halves):
    return jnp.tanh(halves.astype(BF16)) + 1.0


def key_state(keys, values, mask_row):
    width = keys.shape[-1]
    depth = width // HEADS
    turned = values.T * mask_row
    ones = jnp.broadcast_to(mask_row, (16, mask_row.shape[-1]))
    full = jnp.dot(jnp.concatenate([turned, ones], axis=0), keys, preferred_element_type=F32)
    lane_head = lax.broadcasted_iota(jnp.int32, (depth, width), 1) // depth
    packed = jnp.zeros((depth, width), F32)
    for head in range(HEADS):
        packed = jnp.where(lane_head == head, full[head * depth : (head + 1) * depth], packed)
    return packed, full[width : width + 1]


def key_states(keys, values, mask_row, block, inner):
    pick = lambda part, n: part[n * inner : (n + 1) * inner].astype(BF16)
    return [key_state(pick(keys, n), pick(values, n), mask_row) for n in range(block)]


def fill_block_mask(block_mask):
    double, width = block_mask.shape
    depth = width // HEADS
    row_head = lax.broadcasted_iota(jnp.int32, (double, width), 0) // depth % HEADS
    lane_head = lax.broadcasted_iota(jnp.int32, (double, width), 1) // depth
    block_mask[...] = jnp.where(row_head == lane_head, 1.0, 0.0).astype(BF16)


def attend(queries, packed, totals, block_mask):
    width = queries.shape[-1]
    spread = jnp.concatenate([packed] * HEADS, axis=0)
    right = jnp.concatenate([spread, jnp.broadcast_to(totals, (width, width))], axis=0)
    both = lax.dot_general(queries, right * block_mask, NT, preferred_element_type=F32)
    return both[:, :width] / jnp.maximum(both[:, width:], 1.0)


def head_norm(attended, gain, gate):
    width = attended.shape[-1]
    square = jnp.sum(attended * attended, axis=-1, keepdims=True)
    scaled = attended * lax.rsqrt(square + EPSILON * width) * (gain * (0.5 * math.sqrt(width)))
    return (scaled * gate).astype(BF16)


def start_kernel(where, mask, pair, line, gain, w_in, query_out, gate_out, state_out, total_out):
    rows, cols, width = pair.shape
    base = where[1] * (rows * pl.num_programs(0)) + pl.program_id(0) * rows
    x = norm(pair[...].astype(F32).reshape(rows * cols, width), gain[...])
    w = w_in[...]
    w = jnp.concatenate([w[:, : 3 * width], w[:, 3 * width :] * 0.5], axis=1)
    project = jnp.dot(x, w, preferred_element_type=F32)
    fold = lambda part: part.reshape(rows, cols, width)
    query_out[...] = fold(feature(project[:, :width]))
    gate_out[...] = fold(gating(project[:, 3 * width :]))
    keys = feature(project[:, width : 2 * width])
    values = project[:, 2 * width : 3 * width]
    col_mask = line[0].astype(F32).astype(BF16)
    lines = []
    for r, (packed, totals) in enumerate(key_states(keys, values, col_mask, rows, cols)):
        valid = mask[base + r].astype(F32)
        state_out[r] = (packed * valid).astype(BF16)
        lines.append(totals * valid)
    total_out[...] = jnp.concatenate(lines, axis=0).astype(BF16)


def middle_kernel(
    steps,
    part,
    where,
    mask,
    pair,
    query,
    gate,
    state_a,
    state_b,
    total_a,
    total_b,
    line,
    head_gain,
    w_out,
    gain,
    w_key,
    w_value,
    *rest,
):
    update_out, normed_out, state_out, anchor, held, block_mask, *landed, arrived = rest[-12:]
    block_rows, cols, width = update_out.shape
    block_cols, rows, _ = normed_out.shape
    slots, share, depth, _ = state_out.shape
    share = cols // slots
    step = pl.program_id(0)

    def fetches(index):
        some = pl.ds(index * block_rows, block_rows)
        own = pl.ds(part * cols, cols)
        sources = [n.at[some, own] for n in (query, gate, pair)]
        sources += [n.at[some] for n in (state_a, state_b)]
        return [
            pltpu.make_async_copy(source, target.at[some], arrived.at[index, n])
            for n, (source, target) in enumerate(zip(sources, landed))
        ]

    @pl.when(step == 0)
    def _():
        for index in range(steps):
            for fetch in fetches(index):
                fetch.start()
        fill_block_mask(block_mask)

    @pl.when(step < steps)
    def _():
        for fetch in fetches(step):
            fetch.wait()
        some = pl.ds(step * block_rows, block_rows)
        queries, gates, pairs = (n[some] for n in landed[:3])
        mine, others = (n[some].astype(F32) for n in landed[3:])
        both = (mine + others).astype(BF16)
        lines = (total_a[some].astype(F32) + total_b[some].astype(F32)).astype(BF16)
        attended = []
        for r in range(block_rows):
            attended.append(attend(queries[r], both[r], lines[r : r + 1], block_mask[...]))
        flat = (block_rows * cols, width)
        attended = jnp.concatenate(attended, axis=0)
        scaled = head_norm(attended, head_gain[...], gates.astype(F32).reshape(flat))
        update = jnp.dot(scaled, w_out[...], preferred_element_type=F32).astype(BF16)
        update_out[...] = update.reshape(block_rows, cols, width)
        first = pairs.astype(F32).reshape(flat) + update.astype(F32)
        anchor[pl.ds(step * block_rows * cols, block_rows * cols), :] = first

    @pl.when(step >= steps)
    def _():
        base = (step - steps) * block_cols
        first = [anchor[pl.ds(base + c, rows, stride=cols), :] for c in range(block_cols)]
        x = norm(jnp.concatenate(first, axis=0), gain[...])
        normed_out[...] = x.reshape(block_cols, rows, width)
        w = jnp.concatenate([w_key[...], w_value[...]], axis=1)
        project = jnp.dot(x, w, preferred_element_type=F32)
        keys, values = feature(project[:, :width]), project[:, width:]
        row_mask = line[0].astype(F32).astype(BF16)
        offset = where[0] * (mask.shape[0] // where[2]) + part * cols
        for c, (packed, totals) in enumerate(
            key_states(keys, values, row_mask, block_cols, rows)
        ):
            place = base + c
            valid = mask[offset + place].astype(F32)
            state_out[place // share, place % share] = (packed * valid).astype(BF16)
            held[pl.ds(place, 1), :] = totals * valid

    @pl.when(step == pl.num_programs(0) - 1)
    def _():
        for slot in range(slots):
            for low in range(0, share, depth):
                count = min(depth, share - low)
                lines = held[pl.ds(slot * share + low, count), :]
                lines = jnp.concatenate([lines, jnp.zeros((depth - count, width), F32)], axis=0)
                state_out[slot, share + low // depth] = lines.astype(BF16)


def query_kernel(normed, w_query, w_gate, query_out, gate_out):
    cols, rows, width = normed.shape
    x = normed[...].astype(F32).reshape(cols * rows, width).astype(BF16)
    w = jnp.concatenate([w_query[...], w_gate[...] * 0.5], axis=1)
    project = jnp.dot(x, w, preferred_element_type=F32)
    fold = lambda part: part.astype(F32).reshape(cols, rows, width).astype(BF16)
    query_out[...] = fold(feature(project[:, :width]))
    gate_out[...] = fold(gating(project[:, width:]))


def end_kernel(
    pair,
    update_start,
    query,
    gate,
    state,
    head_gain,
    w_out,
    gain,
    w_in,
    w_down,
    *rest,
):
    update_out, trans_out, turned, held, block_mask = rest[-5:]
    rows, block_cols, width = pair.shape
    hidden = w_down.shape[0]
    slots, _, depth, _ = state.shape
    share = held.shape[0] // slots
    step = pl.program_id(0)

    @pl.when(step == 0)
    def _():
        fill_block_mask(block_mask)
        for slot in range(slots):
            for low in range(0, share, depth):
                count = min(depth, share - low)
                lines = state[slot, share + low // depth].astype(F32)[:count]
                held[pl.ds(slot * share + low, count), :] = lines

    attended = []
    for c in range(block_cols):
        place = step * block_cols + c
        packed = state[place // share, place % share]
        totals = held[pl.ds(place, 1), :].astype(BF16)
        attended.append(attend(query[c], packed, totals, block_mask[...]))
    flat = (rows * block_cols, width)
    attended = jnp.concatenate(attended, axis=0)
    scaled = head_norm(attended, head_gain[...], gate[...].astype(F32).reshape(flat))
    update = jnp.dot(scaled, w_out[...], preferred_element_type=F32)
    for c in range(block_cols):
        turned[pl.ds(c, rows, stride=block_cols), :] = update[c * rows : (c + 1) * rows]
    update = turned[...].astype(BF16)
    update_out[...] = update.reshape(rows, block_cols, width)
    first = pair[...].astype(F32) + update_start[...].astype(F32)
    x = norm(first.reshape(flat) + update.astype(F32), gain[...])
    w = w_in[...]
    w = jnp.concatenate([w[:, :hidden] * 0.5, w[:, hidden:]], axis=1)
    lifted = jnp.dot(x, w, preferred_element_type=F32).astype(BF16)
    half = lifted[:, :hidden]
    inner = half * (jnp.tanh(half) + 1.0) * lifted[:, hidden:]
    down = jnp.dot(inner, w_down[...], preferred_element_type=F32)
    trans_out[...] = down.reshape(rows, block_cols, width).astype(BF16)


def column_sum(state):
    size = lax.axis_size("col")
    me = lax.axis_index("col")
    swap = lambda part, bit: lax.ppermute(part, "col", [(n, n ^ bit) for n in range(size)])
    bits = [1 << n for n in range(size.bit_length() - 1)]
    for bit in bits:
        half = state.shape[0] // 2
        side = (me // bit) % 2
        send = lax.dynamic_slice_in_dim(state, (1 - side) * half, half)
        keep = lax.dynamic_slice_in_dim(state, side * half, half)
        other = yield send, swap(send, bit)
        state = (keep.astype(F32) + other.astype(F32)).astype(BF16)
    for bit in reversed(bits):
        other = yield state, swap(state, bit)
        side = (me // bit) % 2
        state = jnp.where(
            side == 0,
            jnp.concatenate([state, other], axis=0),
            jnp.concatenate([other, state], axis=0),
        )
    yield state, None


def whole(shape):
    return pl.BlockSpec(shape, lambda *_: (0,) * len(shape), pipeline_mode=pl.Buffered(1))


def shards(
    pair,
    token_mask,
    start_gain,
    start_head_gain,
    start_in,
    start_out,
    end_gain,
    end_head_gain,
    end_in,
    end_out,
    trans_gain,
    trans_in,
    trans_out,
):
    rows, cols, width = pair.shape
    depth = width // HEADS
    hidden = trans_out.shape[0]
    slots = lax.axis_size("col")
    where = jnp.stack(
        [lax.axis_index("row"), lax.axis_index("col"), jnp.int32(lax.axis_size("row"))]
    ).astype(jnp.int32)
    col_lines = token_mask.reshape(-1, 1, cols)
    row_lines = token_mask.reshape(-1, 1, rows)
    line = lambda gain: gain[None, :]

    tall = math.gcd(rows, 16)
    shape = jax.ShapeDtypeStruct
    block = lambda *dims: pl.BlockSpec(dims, lambda n, *_: (n,) + (0,) * (len(dims) - 1))
    query, gate, state, total = pl.pallas_call(
        start_kernel,
        grid_spec=pltpu.PrefetchScalarGridSpec(
            num_scalar_prefetch=2,
            grid=(rows // tall,),
            in_specs=[
                block(tall, cols, width),
                pl.BlockSpec((1, 1, cols), lambda n, where, mask: (where[0], 0, 0)),
                whole((1, width)),
                whole((width, 4 * width)),
            ],
            out_specs=[
                block(tall, cols, width),
                block(tall, cols, width),
                block(tall, depth, width),
                block(tall, width),
            ],
        ),
        out_shape=[
            shape((rows, cols, width), BF16),
            shape((rows, cols, width), BF16),
            shape((rows, depth, width), BF16),
            shape((rows, width), BF16),
        ],
        compiler_params=params(),
        cost_estimate=cost(rows * cols, 6 * width * width),
        name="start",
    )(where, token_mask, pair, col_lines, line(start_gain), start_in)

    swap = [(n, lax.axis_size("row") - 1 - n) for n in range(lax.axis_size("row"))]
    state_b = lax.ppermute(state, "row", swap)
    total_b = lax.ppermute(total, "row", swap)

    chunk = cols // CHUNKS
    wide = 16
    broad = math.gcd(rows, 16)
    steps = rows // broad
    turns = chunk // wide
    span = chunk // 2
    share = chunk // slots
    slabs = (slots, share + pl.cdiv(share, depth), depth, width)

    column = lambda n: pl.BlockSpec(
        (width, width), lambda *_: (0, n), pipeline_mode=pl.Buffered(1)
    )

    def middle(part, update, gain):
        low = lambda n: jnp.minimum(n, steps - 1)
        high = lambda n: jnp.maximum(n - steps, 0)
        tile = pl.BlockSpec((broad, chunk, width), lambda n, *_: (low(n), part, 0))
        by_col = lambda *dims: pl.BlockSpec(dims, lambda n, *_: (high(n), 0, 0))
        extra = [] if update is None else [update]
        return pl.pallas_call(
            functools.partial(middle_kernel, steps, part),
            grid_spec=pltpu.PrefetchScalarGridSpec(
                num_scalar_prefetch=2,
                grid=(steps + chunk // span,),
                in_specs=[
                    *[pl.BlockSpec(memory_space=pl.ANY)] * 5,
                    whole((rows, width)),
                    whole((rows, width)),
                    pl.BlockSpec((1, 1, rows), lambda n, where, mask: (where[1], 0, 0)),
                    whole((1, width)),
                    whole((width, width)),
                    whole((1, width)),
                    column(1),
                    column(2),
                ]
                + [pl.BlockSpec(memory_space=pl.ANY)] * len(extra),
                out_specs=[
                    tile,
                    by_col(span, rows, width),
                    pl.BlockSpec(slabs, lambda *_: (0, 0, 0, 0)),
                ],
                scratch_shapes=[
                    pltpu.VMEM((rows * chunk, width), F32),
                    pltpu.VMEM((chunk, width), F32),
                    pltpu.VMEM((2 * width, width), BF16),
                    *[pltpu.VMEM((rows, chunk, width), BF16)] * 3,
                    *[pltpu.VMEM((rows, depth, width), BF16)] * 2,
                    pltpu.SemaphoreType.DMA((steps, 5)),
                ],
            ),
            out_shape=[
                shape((rows, cols, width), BF16),
                shape((chunk, rows, width), BF16),
                shape(slabs, BF16),
            ],
            input_output_aliases={15: 0} if extra else {},
            compiler_params=params(),
            cost_estimate=cost(rows * chunk, 7 * width * width),
            name="middle",
        )(
            where,
            token_mask,
            pair,
            query,
            gate,
            state,
            state_b,
            total,
            total_b,
            row_lines,
            line(start_head_gain),
            start_out,
            gain,
            end_in,
            end_in,
            *extra,
        )

    def queries(normed):
        return pl.pallas_call(
            query_kernel,
            grid=(turns,),
            in_specs=[block(wide, rows, width), column(0), column(3)],
            out_specs=[block(wide, rows, width)] * 2,
            out_shape=[shape((chunk, rows, width), BF16)] * 2,
            compiler_params=params(),
            cost_estimate=cost(rows * chunk, 2 * width * width),
            name="queries",
        )(normed, end_in, end_in)

    def end(part, update_start, parts, outs, gain):
        offset = part * turns
        tile = pl.BlockSpec((rows, wide, width), lambda n: (0, offset + n, 0))
        return pl.pallas_call(
            end_kernel,
            grid=(turns,),
            in_specs=[
                tile,
                tile,
                block(wide, rows, width),
                block(wide, rows, width),
                whole(slabs),
                whole((1, width)),
                whole((width, width)),
                whole((1, width)),
                whole((width, 2 * hidden)),
                whole((hidden, width)),
            ]
            + [pl.BlockSpec(memory_space=pl.ANY)] * len(outs),
            out_specs=[tile, tile],
            scratch_shapes=[
                pltpu.VMEM((rows * wide, width), F32),
                pltpu.VMEM((chunk, width), F32),
                pltpu.VMEM((2 * width, width), BF16),
            ],
            out_shape=[shape((rows, cols, width), BF16)] * 2,
            input_output_aliases={10: 0, 11: 1} if outs else {},
            compiler_params=params(),
            cost_estimate=cost(rows * chunk, 2 * width * width + 3 * width * hidden),
            name="end",
        )(
            pair,
            update_start,
            *parts,
            line(end_head_gain),
            end_out,
            gain,
            trans_in,
            trans_out,
            *outs,
        )

    sums = []
    latest = []

    def advance(done):
        live = [n for n, (_, other) in enumerate(latest) if other is not None]
        if not live:
            return done, []
        done, *others = lax.optimization_barrier((done, *(latest[n][1] for n in live)))
        for n, other in zip(live, others):
            latest[n] = sums[n].send(other)
        return done, [*others, *(latest[n][0] for n in live)]

    def after(value, behind):
        return lax.optimization_barrier((value, *behind))[0] if behind else value

    update_start = None
    outs = ()
    held = []
    behind = []
    for part in range(CHUNKS):
        update_start, normed, state_e = middle(part, update_start, after(line(end_gain), behind))
        held.append(normed)
        state_e, behind = advance(state_e)
        sums.append(column_sum(state_e))
        latest.append(next(sums[-1]))
        behind.append(latest[-1][0])
    waiting = list(range(CHUNKS))
    for part in range(CHUNKS):
        while latest[part][1] is not None:
            batch = waiting[: 2 if len(waiting) > 2 else 1]
            waiting = waiting[len(batch) :]
            for n in batch:
                held[n] = queries(after(held[n], behind))
            if batch:
                first, behind = advance(held[batch[-1]][0])
                held[batch[-1]] = (first, held[batch[-1]][1])
            else:
                _, behind = advance(line(trans_gain))
        for n in waiting:
            held[n] = queries(held[n])
        waiting = []
        gain = after(line(trans_gain), behind)
        outs = end(part, update_start, (*held[part], latest[part][0]), outs, gain)
        first, behind = advance(outs[0])
        outs = (first, outs[1])
    return (update_start, outs[0], outs[1])


def solution(mesh):
    pair_spec = P(("groups", "col"), "row", None)
    return jax.shard_map(
        shards,
        mesh=mesh,
        in_specs=(pair_spec, P("groups")) + (P(),) * 11,
        out_specs=(pair_spec,) * 3,
        check_vma=False,
    )
```

```python
import functools
import math

import jax
import jax.numpy as jnp
from jax import lax
from jax.experimental import pallas as pl
from jax.experimental.pallas import tpu as pltpu
from jax.sharding import PartitionSpec as P

HEADS = 4
EPSILON = 1e-05
BF16 = jnp.bfloat16
F32 = jnp.float32
NT = (((1,), (1,)), ((), ()))


def params():
    return pltpu.CompilerParams(
        dimension_semantics=("arbitrary",),
        vmem_limit_bytes=56 * 1024 * 1024,
    )


def cost(pairs, products):
    return pl.CostEstimate(
        flops=16 * pairs * products, transcendentals=0, bytes_accessed=64 * pairs
    )


def norm(values, gain):
    width = values.shape[-1]
    centered = values - jnp.sum(values, axis=-1, keepdims=True) * (1.0 / width)
    square = jnp.sum(centered * centered, axis=-1, keepdims=True)
    return (centered * lax.rsqrt(square + EPSILON * width) * (gain * math.sqrt(width))).astype(BF16)


def feature(values):
    values = values.astype(BF16)
    return jnp.where(values > 0, values + 1.0, jnp.exp(values))


def gating(halves):
    return jnp.tanh(halves.astype(BF16)) + 1.0


def key_state(keys, values, mask_row):
    width = keys.shape[-1]
    depth = width // HEADS
    turned = values.T * mask_row
    ones = jnp.broadcast_to(mask_row, (16, mask_row.shape[-1]))
    full = jnp.dot(jnp.concatenate([turned, ones], axis=0), keys, preferred_element_type=F32)
    lane_head = lax.broadcasted_iota(jnp.int32, (depth, width), 1) // depth
    packed = jnp.zeros((depth, width), F32)
    for head in range(HEADS):
        packed = jnp.where(lane_head == head, full[head * depth : (head + 1) * depth], packed)
    return packed, full[width : width + 1]


def key_states(keys, values, mask_row, block, inner):
    pick = lambda part, n: part[n * inner : (n + 1) * inner].astype(BF16)
    return [key_state(pick(keys, n), pick(values, n), mask_row) for n in range(block)]


def fill_block_mask(block_mask):
    double, width = block_mask.shape
    depth = width // HEADS
    row_head = lax.broadcasted_iota(jnp.int32, (double, width), 0) // depth % HEADS
    lane_head = lax.broadcasted_iota(jnp.int32, (double, width), 1) // depth
    block_mask[...] = jnp.where(row_head == lane_head, 1.0, 0.0).astype(BF16)


def attend(queries, packed, totals, block_mask):
    width = queries.shape[-1]
    spread = jnp.concatenate([packed] * HEADS, axis=0)
    right = jnp.concatenate([spread, jnp.broadcast_to(totals, (width, width))], axis=0)
    both = lax.dot_general(queries, right * block_mask, NT, preferred_element_type=F32)
    return both[:, :width] / jnp.maximum(both[:, width:], 1.0)


def head_norm(attended, gain, gate):
    width = attended.shape[-1]
    square = jnp.sum(attended * attended, axis=-1, keepdims=True)
    scaled = attended * lax.rsqrt(square + EPSILON * width) * (gain * (0.5 * math.sqrt(width)))
    return (scaled * gate).astype(BF16)


def start_kernel(where, mask, pair, line, gain, w_in, query_out, gate_out, state_out, total_out):
    rows, cols, width = pair.shape
    base = where[1] * (rows * pl.num_programs(0)) + pl.program_id(0) * rows
    x = norm(pair[...].astype(F32).reshape(rows * cols, width), gain[...])
    w = w_in[...]
    w = jnp.concatenate([w[:, : 3 * width], w[:, 3 * width :] * 0.5], axis=1)
    project = jnp.dot(x, w, preferred_element_type=F32)
    fold = lambda part: part.reshape(rows, cols, width)
    query_out[...] = fold(feature(project[:, :width]))
    gate_out[...] = fold(gating(project[:, 3 * width :]))
    keys = feature(project[:, width : 2 * width])
    values = project[:, 2 * width : 3 * width]
    col_mask = line[0].astype(F32).astype(BF16)
    lines = []
    for r, (packed, totals) in enumerate(key_states(keys, values, col_mask, rows, cols)):
        valid = mask[base + r].astype(F32)
        state_out[r] = (packed * valid).astype(BF16)
        lines.append(totals * valid)
    total_out[...] = jnp.concatenate(lines, axis=0).astype(BF16)


def middle_kernel(
    steps,
    offset,
    where,
    mask,
    pair,
    query,
    gate,
    state_a,
    state_b,
    total_a,
    total_b,
    line,
    head_gain,
    w_out,
    gain,
    w_key,
    w_value,
    *rest,
):
    update_out, normed_out, send_out, keep_out, anchor, held, block_mask, staged = rest[-14:-6]
    *landed, arrived = rest[-6:]
    block_rows, cols, width = update_out.shape
    block_cols, rows, _ = normed_out.shape
    _, half, _, depth, _ = staged.shape
    share, room = cols // (2 * half), held.shape[0] // (2 * half)
    step = pl.program_id(0)
    side = where[1] % 2
    spot = lambda slot: (1 - jnp.abs(slot // half - side), slot % half)

    def fetches(index):
        some = pl.ds(index * block_rows, block_rows)
        own = pl.ds(offset, cols)
        sources = [n.at[some, own] for n in (query, gate, pair)]
        sources += [n.at[some] for n in (state_a, state_b)]
        return [
            pltpu.make_async_copy(source, target.at[some], arrived.at[index, n])
            for n, (source, target) in enumerate(zip(sources, landed))
        ]

    @pl.when(step == 0)
    def _():
        for index in range(steps):
            for fetch in fetches(index):
                fetch.start()
        fill_block_mask(block_mask)
        held[...] = jnp.zeros_like(held)

    @pl.when(step < steps)
    def _():
        for fetch in fetches(step):
            fetch.wait()
        some = pl.ds(step * block_rows, block_rows)
        queries, gates, pairs = (n[some] for n in landed[:3])
        mine, others = (n[some].astype(F32) for n in landed[3:])
        both = (mine + others).astype(BF16)
        lines = (total_a[some].astype(F32) + total_b[some].astype(F32)).astype(BF16)
        attended = []
        for r in range(block_rows):
            attended.append(attend(queries[r], both[r], lines[r : r + 1], block_mask[...]))
        flat = (block_rows * cols, width)
        attended = jnp.concatenate(attended, axis=0)
        scaled = head_norm(attended, head_gain[...], gates.astype(F32).reshape(flat))
        update = jnp.dot(scaled, w_out[...], preferred_element_type=F32).astype(BF16)
        update_out[...] = update.reshape(block_rows, cols, width)
        first = pairs.astype(F32).reshape(flat) + update.astype(F32)
        anchor[pl.ds(step * block_rows * cols, block_rows * cols), :] = first

    @pl.when(step >= steps)
    def _():
        base = (step - steps) * block_cols
        first = [anchor[pl.ds(base + c, rows, stride=cols), :] for c in range(block_cols)]
        x = norm(jnp.concatenate(first, axis=0), gain[...])
        normed_out[...] = x.reshape(block_cols, rows, width)
        w = jnp.concatenate([w_key[...], w_value[...]], axis=1)
        project = jnp.dot(x, w, preferred_element_type=F32)
        keys, values = feature(project[:, :width]), project[:, width:]
        row_mask = line[0].astype(F32).astype(BF16)
        start = where[0] * (mask.shape[0] // where[2]) + offset
        for c, (packed, totals) in enumerate(
            key_states(keys, values, row_mask, block_cols, rows)
        ):
            place = base + c
            valid = mask[start + place].astype(F32)
            staged[*spot(place // share), place % share] = (packed * valid).astype(BF16)
            held[pl.ds(place // share * room + place % share, 1), :] = totals * valid

    @pl.when(step == pl.num_programs(0) - 1)
    def _():
        for slot in range(2 * half):
            for low in range(0, room, depth):
                lines = held[pl.ds(slot * room + low, depth), :].astype(BF16)
                staged[*spot(slot), share + low // depth] = lines
        send_out[...] = staged[0]
        keep_out[...] = staged[1]


def query_kernel(normed, w_query, w_gate, query_out, gate_out):
    cols, rows, width = normed.shape
    x = normed[...].astype(F32).reshape(cols * rows, width).astype(BF16)
    w = jnp.concatenate([w_query[...], w_gate[...] * 0.5], axis=1)
    project = jnp.dot(x, w, preferred_element_type=F32)
    fold = lambda part: part.astype(F32).reshape(cols, rows, width).astype(BF16)
    query_out[...] = fold(feature(project[:, :width]))
    gate_out[...] = fold(gating(project[:, width:]))


def end_kernel(
    where,
    pair,
    update_start,
    query,
    gate,
    mine,
    other,
    head_gain,
    w_out,
    gain,
    w_in,
    w_down,
    *rest,
):
    update_out, trans_out, turned, held, block_mask, state = rest[-6:]
    rows, block_cols, width = pair.shape
    hidden = w_down.shape[0]
    _, half, _, depth, _ = state.shape
    share = pl.num_programs(0) * block_cols // (2 * half)
    room = held.shape[0] // (2 * half)
    step = pl.program_id(0)

    @pl.when(step == 0)
    def _():
        fill_block_mask(block_mask)
        side = where[1] % 2
        state[side] = mine[...]
        state[1 - side] = other[...]
        for slot in range(2 * half):
            for low in range(0, room, depth):
                lines = state[slot // half, slot % half, share + low // depth].astype(F32)
                held[pl.ds(slot * room + low, depth), :] = lines

    attended = []
    for c in range(block_cols):
        place = step * block_cols + c
        slot = place // share
        packed = state[slot // half, slot % half, place % share]
        totals = held[pl.ds(slot * room + place % share, 1), :].astype(BF16)
        attended.append(attend(query[c], packed, totals, block_mask[...]))
    flat = (rows * block_cols, width)
    attended = jnp.concatenate(attended, axis=0)
    scaled = head_norm(attended, head_gain[...], gate[...].astype(F32).reshape(flat))
    update = jnp.dot(scaled, w_out[...], preferred_element_type=F32)
    for c in range(block_cols):
        turned[pl.ds(c, rows, stride=block_cols), :] = update[c * rows : (c + 1) * rows]
    update = turned[...].astype(BF16)
    update_out[...] = update.reshape(rows, block_cols, width)
    first = pair[...].astype(F32) + update_start[...].astype(F32)
    x = norm(first.reshape(flat) + update.astype(F32), gain[...])
    w = w_in[...]
    w = jnp.concatenate([w[:, :hidden] * 0.5, w[:, hidden:]], axis=1)
    lifted = jnp.dot(x, w, preferred_element_type=F32).astype(BF16)
    half = lifted[:, :hidden]
    inner = half * (jnp.tanh(half) + 1.0) * lifted[:, hidden:]
    down = jnp.dot(inner, w_down[...], preferred_element_type=F32)
    trans_out[...] = down.reshape(rows, block_cols, width).astype(BF16)


def column_sum(send, keep):
    size = lax.axis_size("col")
    swap = lambda part, bit: lax.ppermute(part, "col", [(n, n ^ bit) for n in range(size)])
    add = lambda one, two: (one.astype(F32) + two.astype(F32)).astype(BF16)
    other = yield send, swap(send, 1)
    state = add(keep, other)
    for bit in [1 << n for n in range(1, size.bit_length() - 1)]:
        other = yield state, swap(state, bit)
        state = add(state, other)
    other = yield state, swap(state, 1)
    yield (state, other), None


def column_chunks(cols, slots):
    count = 4
    while count > 1 and (cols % count or cols // count % 16 or cols // count % slots):
        count -= 1
    return [(n * (cols // count), cols // count) for n in range(count)]


def whole(shape):
    return pl.BlockSpec(shape, lambda *_: (0,) * len(shape), pipeline_mode=pl.Buffered(1))


def shards(
    pair,
    token_mask,
    start_gain,
    start_head_gain,
    start_in,
    start_out,
    end_gain,
    end_head_gain,
    end_in,
    end_out,
    trans_gain,
    trans_in,
    trans_out,
):
    rows, cols, width = pair.shape
    depth = width // HEADS
    hidden = trans_out.shape[0]
    slots = 2
    where = jnp.stack(
        [lax.axis_index("row"), lax.axis_index("col"), jnp.int32(lax.axis_size("row"))]
    ).astype(jnp.int32)
    col_lines = token_mask.reshape(-1, 1, cols)
    row_lines = token_mask.reshape(-1, 1, rows)
    line = lambda gain: gain[None, :]

    tall = math.gcd(rows, 16)
    shape = jax.ShapeDtypeStruct
    block = lambda *dims: pl.BlockSpec(dims, lambda n, *_: (n,) + (0,) * (len(dims) - 1))
    query, gate, state, total = pl.pallas_call(
        start_kernel,
        grid_spec=pltpu.PrefetchScalarGridSpec(
            num_scalar_prefetch=2,
            grid=(rows // tall,),
            in_specs=[
                block(tall, cols, width),
                pl.BlockSpec((1, 1, cols), lambda n, where, mask: (where[0], 0, 0)),
                whole((1, width)),
                whole((width, 4 * width)),
            ],
            out_specs=[
                block(tall, cols, width),
                block(tall, cols, width),
                block(tall, depth, width),
                block(tall, width),
            ],
        ),
        out_shape=[
            shape((rows, cols, width), BF16),
            shape((rows, cols, width), BF16),
            shape((rows, depth, width), BF16),
            shape((rows, width), BF16),
        ],
        compiler_params=params(),
        cost_estimate=cost(rows * cols, 6 * width * width),
        name="start",
    )(where, token_mask, pair, col_lines, line(start_gain), start_in)

    swap = [(n, lax.axis_size("row") - 1 - n) for n in range(lax.axis_size("row"))]
    state_b = lax.ppermute(state, "row", swap)
    total_b = lax.ppermute(total, "row", swap)

    wide = 16
    broad = math.gcd(rows, 16)
    steps = rows // broad
    chunks = column_chunks(cols, slots)
    extra_slabs = [pl.cdiv(size // slots, depth) for _, size in chunks]
    rooms = [slots * depth * more for more in extra_slabs]
    slabs = [
        (slots // 2, size // slots + more, depth, width)
        for (_, size), more in zip(chunks, extra_slabs)
    ]

    column = lambda n: pl.BlockSpec(
        (width, width), lambda *_: (0, n), pipeline_mode=pl.Buffered(1)
    )

    def middle(part, update, gain):
        offset, chunk = chunks[part]
        span = chunk // 2
        low = lambda n: jnp.minimum(n, steps - 1)
        high = lambda n: jnp.maximum(n - steps, 0)
        tile = pl.BlockSpec((broad, chunk, width), lambda n, *_: (low(n), offset // chunk, 0))
        by_col = lambda *dims: pl.BlockSpec(dims, lambda n, *_: (high(n), 0, 0))
        extra = [] if update is None else [update]
        return pl.pallas_call(
            functools.partial(middle_kernel, steps, offset),
            grid_spec=pltpu.PrefetchScalarGridSpec(
                num_scalar_prefetch=2,
                grid=(steps + chunk // span,),
                in_specs=[
                    *[pl.BlockSpec(memory_space=pl.ANY)] * 5,
                    whole((rows, width)),
                    whole((rows, width)),
                    pl.BlockSpec((1, 1, rows), lambda n, where, mask: (where[1], 0, 0)),
                    whole((1, width)),
                    whole((width, width)),
                    whole((1, width)),
                    column(1),
                    column(2),
                ]
                + [pl.BlockSpec(memory_space=pl.ANY)] * len(extra),
                out_specs=[
                    tile,
                    by_col(span, rows, width),
                    *[pl.BlockSpec(slabs[part], lambda *_: (0, 0, 0, 0))] * 2,
                ],
                scratch_shapes=[
                    pltpu.VMEM((rows * chunk, width), F32),
                    pltpu.VMEM((rooms[part], width), F32),
                    pltpu.VMEM((2 * width, width), BF16),
                    pltpu.VMEM((2, *slabs[part]), BF16),
                    *[pltpu.VMEM((rows, chunk, width), BF16)] * 3,
                    *[pltpu.VMEM((rows, depth, width), BF16)] * 2,
                    pltpu.SemaphoreType.DMA((steps, 5)),
                ],
            ),
            out_shape=[
                shape((rows, cols, width), BF16),
                shape((chunk, rows, width), BF16),
                *[shape(slabs[part], BF16)] * 2,
            ],
            input_output_aliases={15: 0} if extra else {},
            compiler_params=params(),
            cost_estimate=cost(rows * chunk, 7 * width * width),
            name="middle",
        )(
            where,
            token_mask,
            pair,
            query,
            gate,
            state,
            state_b,
            total,
            total_b,
            row_lines,
            line(start_head_gain),
            start_out,
            gain,
            end_in,
            end_in,
            *extra,
        )

    def queries(normed):
        chunk = normed.shape[0]
        span = chunk // 2
        return pl.pallas_call(
            query_kernel,
            grid=(chunk // span,),
            in_specs=[block(span, rows, width), column(0), column(3)],
            out_specs=[block(span, rows, width)] * 2,
            out_shape=[shape((chunk, rows, width), BF16)] * 2,
            compiler_params=params(),
            cost_estimate=cost(rows * chunk, 2 * width * width),
            name="queries",
        )(normed, end_in, end_in)

    def end(part, update_start, parts, outs, gain):
        offset, chunk = chunks[part]
        tile = pl.BlockSpec((rows, wide, width), lambda n, *_: (0, offset // wide + n, 0))
        return pl.pallas_call(
            end_kernel,
            grid_spec=pltpu.PrefetchScalarGridSpec(
                num_scalar_prefetch=1,
                grid=(chunk // wide,),
                in_specs=[
                    tile,
                    tile,
                    block(wide, rows, width),
                    block(wide, rows, width),
                    whole(slabs[part]),
                    whole(slabs[part]),
                    whole((1, width)),
                    whole((width, width)),
                    whole((1, width)),
                    whole((width, 2 * hidden)),
                    whole((hidden, width)),
                ]
                + [pl.BlockSpec(memory_space=pl.ANY)] * len(outs),
                out_specs=[tile, tile],
                scratch_shapes=[
                    pltpu.VMEM((rows * wide, width), F32),
                    pltpu.VMEM((rooms[part], width), F32),
                    pltpu.VMEM((2 * width, width), BF16),
                    pltpu.VMEM((2, *slabs[part]), BF16),
                ],
            ),
            out_shape=[shape((rows, cols, width), BF16)] * 2,
            input_output_aliases={12: 0, 13: 1} if outs else {},
            compiler_params=params(),
            cost_estimate=cost(rows * chunk, 2 * width * width + 3 * width * hidden),
            name="end",
        )(
            where,
            pair,
            update_start,
            *parts,
            line(end_head_gain),
            end_out,
            gain,
            trans_in,
            trans_out,
            *outs,
        )

    sums = []
    latest = []

    def advance(done):
        live = [n for n, (_, other) in enumerate(latest) if other is not None]
        if not live:
            return done, []
        done, *others = lax.optimization_barrier((done, *(latest[n][1] for n in live)))
        for n, other in zip(live, others):
            latest[n] = sums[n].send(other)
        return done, [*others, *jax.tree.leaves([latest[n][0] for n in live])]

    def after(value, behind):
        return lax.optimization_barrier((value, *behind))[0] if behind else value

    update_start = None
    outs = ()
    held = []
    behind = []
    for part in range(len(chunks)):
        update_start, normed, send, keep = middle(
            part, update_start, after(line(end_gain), behind)
        )
        held.append(normed)
        send, behind = advance(send)
        sums.append(column_sum(send, keep))
        latest.append(next(sums[-1]))
        behind.append(latest[-1][0])
    waiting = list(range(len(chunks)))
    for part in range(len(chunks)):
        while latest[part][1] is not None:
            batch = waiting
            waiting = waiting[len(batch) :]
            for n in batch:
                held[n] = queries(after(held[n], behind))
            if batch:
                first, behind = advance(held[batch[-1]][0])
                held[batch[-1]] = (first, held[batch[-1]][1])
            else:
                _, behind = advance(line(trans_gain))
        for n in waiting:
            held[n] = queries(held[n])
        waiting = []
        gain = after(line(trans_gain), behind)
        outs = end(part, update_start, (*held[part], *latest[part][0]), outs, gain)
        first, behind = advance(outs[0])
        outs = (first, outs[1])
    return (update_start, outs[0], outs[1])


def solution(mesh):
    pair_spec = P(("groups", "col"), "row", None)
    return jax.shard_map(
        shards,
        mesh=mesh,
        in_specs=(pair_spec, P("groups")) + (P(),) * 11,
        out_specs=(pair_spec,) * 3,
        check_vma=False,
    )
```

```python
import functools
import math

import jax
import jax.numpy as jnp
from jax import lax
from jax.experimental import pallas as pl
from jax.experimental.pallas import tpu as pltpu
from jax.sharding import PartitionSpec as P

HEADS = 4
EPSILON = 1e-05
BF16 = jnp.bfloat16
F32 = jnp.float32
NT = (((1,), (1,)), ((), ()))


def params():
    return pltpu.CompilerParams(
        dimension_semantics=("arbitrary",),
        vmem_limit_bytes=56 * 1024 * 1024,
    )


def cost(pairs, products):
    return pl.CostEstimate(
        flops=16 * pairs * products, transcendentals=0, bytes_accessed=64 * pairs
    )


def square_block(width, centering):
    row = lax.broadcasted_iota(jnp.int32, (2 * width, 2 * width), 0)
    lane = lax.broadcasted_iota(jnp.int32, (2 * width, 2 * width), 1)
    if centering:
        block = jnp.where(row == lane, 1.0 - 1.0 / width, -1.0 / width)
    else:
        block = jnp.ones((2 * width, 2 * width), F32)
    return jnp.where(row // width == lane // width, block, 0.0).astype(BF16)


def paired(values, block):
    half, width = values.shape[0] // 2, values.shape[1]
    sides = jnp.concatenate([values[:half], values[half:]], axis=1)
    both = jnp.dot(sides, block, preferred_element_type=F32)
    return jnp.concatenate([both[:, :width], both[:, width:]], axis=0)


def summed_center(one, two):
    width = one.shape[1]
    center = square_block(width, True)[:width, :width]
    return jnp.dot(
        jnp.concatenate([one, two], axis=1),
        jnp.concatenate([center, center], axis=0),
        preferred_element_type=F32,
    )


def norm(centered, gain):
    width = centered.shape[-1]
    square = paired((centered * centered).astype(BF16), square_block(width, False))
    return (centered * lax.rsqrt(square + EPSILON * width) * (gain * math.sqrt(width))).astype(BF16)


def feature(values):
    values = values.astype(BF16)
    return jnp.where(values > 0, values + 1.0, jnp.exp(values))


def gating(halves):
    return jnp.tanh(halves.astype(BF16)) + 1.0


def key_state(keys, values, mask_row):
    width = keys.shape[-1]
    depth = width // HEADS
    turned = values.T * mask_row
    ones = jnp.broadcast_to(mask_row, (16, mask_row.shape[-1]))
    full = jnp.dot(jnp.concatenate([turned, ones], axis=0), keys, preferred_element_type=F32)
    lane_head = lax.broadcasted_iota(jnp.int32, (depth, width), 1) // depth
    packed = jnp.zeros((depth, width), F32)
    for head in range(HEADS):
        packed = jnp.where(lane_head == head, full[head * depth : (head + 1) * depth], packed)
    return packed, full[width : width + 1]


def key_states(keys, values, mask_row, block, inner):
    pick = lambda part, n: part[n * inner : (n + 1) * inner].astype(BF16)
    return [key_state(pick(keys, n), pick(values, n), mask_row) for n in range(block)]


def fill_block_mask(block_mask):
    double, width = block_mask.shape
    depth = width // HEADS
    row_head = lax.broadcasted_iota(jnp.int32, (double, width), 0) // depth % HEADS
    lane_head = lax.broadcasted_iota(jnp.int32, (double, width), 1) // depth
    block_mask[...] = jnp.where(row_head == lane_head, 1.0, 0.0).astype(BF16)


def attend(queries, packed, totals, block_mask):
    width = queries.shape[-1]
    spread = jnp.concatenate([packed] * HEADS, axis=0)
    right = jnp.concatenate([spread, jnp.broadcast_to(totals, (width, width))], axis=0)
    both = lax.dot_general(queries, right * block_mask, NT, preferred_element_type=F32)
    return both[:, :width] / jnp.maximum(both[:, width:], 1.0)


def head_norm(attended, gain, gate):
    width = attended.shape[-1]
    square = jnp.sum(attended * attended, axis=-1, keepdims=True)
    scaled = attended * lax.rsqrt(square + EPSILON * width) * (gain * (0.5 * math.sqrt(width)))
    return (scaled * gate).astype(BF16)


def start_kernel(where, mask, pair, line, gain, w_in, query_out, gate_out, state_out, total_out):
    rows, cols, width = pair.shape
    base = where[1] * (rows * pl.num_programs(0)) + pl.program_id(0) * rows
    centered = paired(pair[...].reshape(rows * cols, width), square_block(width, True))
    x = norm(centered, gain[...])
    w = w_in[...]
    w = jnp.concatenate([w[:, : 3 * width], w[:, 3 * width :] * 0.5], axis=1)
    project = jnp.dot(x, w, preferred_element_type=F32)
    fold = lambda part: part.reshape(rows, cols, width)
    query_out[...] = fold(feature(project[:, :width]))
    gate_out[...] = fold(gating(project[:, 3 * width :]))
    keys = feature(project[:, width : 2 * width])
    values = project[:, 2 * width : 3 * width]
    col_mask = line[0].astype(F32).astype(BF16)
    lines = []
    for r, (packed, totals) in enumerate(key_states(keys, values, col_mask, rows, cols)):
        valid = mask[base + r].astype(F32)
        state_out[r] = (packed * valid).astype(BF16)
        lines.append(totals * valid)
    total_out[...] = jnp.concatenate(lines, axis=0).astype(BF16)


def middle_kernel(
    steps,
    offset,
    where,
    mask,
    pair,
    query,
    gate,
    state_a,
    state_b,
    total_a,
    total_b,
    line,
    head_gain,
    w_out,
    gain,
    w_key,
    w_value,
    *rest,
):
    update_out, normed_out, send_out, keep_out, anchor, held, block_mask, staged = rest[-14:-6]
    *landed, arrived = rest[-6:]
    block_rows, cols, width = update_out.shape
    block_cols, rows, _ = normed_out.shape
    _, half, _, depth, _ = staged.shape
    share, room = cols // (2 * half), held.shape[0] // (2 * half)
    step = pl.program_id(0)
    side = where[1] % 2
    spot = lambda slot: (1 - jnp.abs(slot // half - side), slot % half)

    def fetches(index):
        some = pl.ds(index * block_rows, block_rows)
        own = pl.ds(offset, cols)
        sources = [n.at[some, own] for n in (query, gate, pair)]
        sources += [n.at[some] for n in (state_a, state_b)]
        return [
            pltpu.make_async_copy(source, target.at[some], arrived.at[index, n])
            for n, (source, target) in enumerate(zip(sources, landed))
        ]

    @pl.when(step == 0)
    def _():
        for index in range(steps):
            for fetch in fetches(index):
                fetch.start()
        fill_block_mask(block_mask)
        held[...] = jnp.zeros_like(held)

    @pl.when(step < steps)
    def _():
        for fetch in fetches(step):
            fetch.wait()
        some = pl.ds(step * block_rows, block_rows)
        queries, gates, pairs = (n[some] for n in landed[:3])
        mine, others = (n[some].astype(F32) for n in landed[3:])
        both = (mine + others).astype(BF16)
        lines = (total_a[some].astype(F32) + total_b[some].astype(F32)).astype(BF16)
        attended = []
        for r in range(block_rows):
            attended.append(attend(queries[r], both[r], lines[r : r + 1], block_mask[...]))
        flat = (block_rows * cols, width)
        attended = jnp.concatenate(attended, axis=0)
        scaled = head_norm(attended, head_gain[...], gates.astype(F32).reshape(flat))
        update = jnp.dot(scaled, w_out[...], preferred_element_type=F32).astype(BF16)
        update_out[...] = update.reshape(block_rows, cols, width)
        centered = summed_center(pairs.reshape(flat), update)
        anchor[pl.ds(step * block_rows * cols, block_rows * cols), :] = centered

    @pl.when(step >= steps)
    def _():
        base = (step - steps) * block_cols
        centered = [anchor[pl.ds(base + c, rows, stride=cols), :] for c in range(block_cols)]
        x = norm(jnp.concatenate(centered, axis=0), gain[...])
        normed_out[...] = x.reshape(block_cols, rows, width)
        w = jnp.concatenate([w_key[...], w_value[...]], axis=1)
        project = jnp.dot(x, w, preferred_element_type=F32)
        keys, values = feature(project[:, :width]), project[:, width:]
        row_mask = line[0].astype(F32).astype(BF16)
        start = where[0] * (mask.shape[0] // where[2]) + offset
        for c, (packed, totals) in enumerate(
            key_states(keys, values, row_mask, block_cols, rows)
        ):
            place = base + c
            valid = mask[start + place].astype(F32)
            staged[*spot(place // share), place % share] = (packed * valid).astype(BF16)
            held[pl.ds(place // share * room + place % share, 1), :] = totals * valid

    @pl.when(step == pl.num_programs(0) - 1)
    def _():
        for slot in range(2 * half):
            for low in range(0, room, depth):
                lines = held[pl.ds(slot * room + low, depth), :].astype(BF16)
                staged[*spot(slot), share + low // depth] = lines
        send_out[...] = staged[0]
        keep_out[...] = staged[1]


def query_kernel(normed, w_query, w_gate, query_out, gate_out):
    cols, rows, width = normed.shape
    x = normed[...].astype(F32).reshape(cols * rows, width).astype(BF16)
    w = jnp.concatenate([w_query[...], w_gate[...] * 0.5], axis=1)
    project = jnp.dot(x, w, preferred_element_type=F32)
    fold = lambda part: part.astype(F32).reshape(cols, rows, width).astype(BF16)
    query_out[...] = fold(feature(project[:, :width]))
    gate_out[...] = fold(gating(project[:, width:]))


def end_kernel(
    where,
    pair,
    update_start,
    query,
    gate,
    mine,
    other,
    head_gain,
    w_out,
    gain,
    w_in,
    w_down,
    *rest,
):
    update_out, trans_out, turned, held, block_mask, state = rest[-6:]
    rows, block_cols, width = pair.shape
    hidden = w_down.shape[0]
    _, half, _, depth, _ = state.shape
    share = pl.num_programs(0) * block_cols // (2 * half)
    room = held.shape[0] // (2 * half)
    step = pl.program_id(0)

    @pl.when(step == 0)
    def _():
        fill_block_mask(block_mask)
        side = where[1] % 2
        state[side] = mine[...]
        state[1 - side] = other[...]
        for slot in range(2 * half):
            for low in range(0, room, depth):
                lines = state[slot // half, slot % half, share + low // depth].astype(F32)
                held[pl.ds(slot * room + low, depth), :] = lines

    attended = []
    for c in range(block_cols):
        place = step * block_cols + c
        slot = place // share
        packed = state[slot // half, slot % half, place % share]
        totals = held[pl.ds(slot * room + place % share, 1), :].astype(BF16)
        attended.append(attend(query[c], packed, totals, block_mask[...]))
    flat = (rows * block_cols, width)
    attended = jnp.concatenate(attended, axis=0)
    scaled = head_norm(attended, head_gain[...], gate[...].astype(F32).reshape(flat))
    update = jnp.dot(scaled, w_out[...], preferred_element_type=F32)
    for c in range(block_cols):
        turned[pl.ds(c, rows, stride=block_cols), :] = update[c * rows : (c + 1) * rows]
    update = turned[...].astype(BF16)
    update_out[...] = update.reshape(rows, block_cols, width)
    first = pair[...].astype(F32) + update_start[...].astype(F32)
    second = first.reshape(flat) + update.astype(F32)
    centered = second - jnp.sum(second, axis=-1, keepdims=True) * (1.0 / width)
    x = norm(centered, gain[...])
    w = w_in[...]
    w = jnp.concatenate([w[:, :hidden] * 0.5, w[:, hidden:]], axis=1)
    lifted = jnp.dot(x, w, preferred_element_type=F32).astype(BF16)
    half = lifted[:, :hidden]
    inner = half * (jnp.tanh(half) + 1.0) * lifted[:, hidden:]
    down = jnp.dot(inner, w_down[...], preferred_element_type=F32)
    trans_out[...] = down.reshape(rows, block_cols, width).astype(BF16)


def column_sum(send, keep):
    size = lax.axis_size("col")
    swap = lambda part, bit: lax.ppermute(part, "col", [(n, n ^ bit) for n in range(size)])
    add = lambda one, two: (one.astype(F32) + two.astype(F32)).astype(BF16)
    other = yield send, swap(send, 1)
    state = add(keep, other)
    for bit in [1 << n for n in range(1, size.bit_length() - 1)]:
        other = yield state, swap(state, bit)
        state = add(state, other)
    other = yield state, swap(state, 1)
    yield (state, other), None


def column_chunks(cols, slots):
    count = 4
    while count > 1 and (cols % count or cols // count % 16 or cols // count % slots):
        count -= 1
    return [(n * (cols // count), cols // count) for n in range(count)]


def whole(shape):
    return pl.BlockSpec(shape, lambda *_: (0,) * len(shape), pipeline_mode=pl.Buffered(1))


def shards(
    pair,
    token_mask,
    start_gain,
    start_head_gain,
    start_in,
    start_out,
    end_gain,
    end_head_gain,
    end_in,
    end_out,
    trans_gain,
    trans_in,
    trans_out,
):
    rows, cols, width = pair.shape
    depth = width // HEADS
    hidden = trans_out.shape[0]
    slots = 2
    where = jnp.stack(
        [lax.axis_index("row"), lax.axis_index("col"), jnp.int32(lax.axis_size("row"))]
    ).astype(jnp.int32)
    col_lines = token_mask.reshape(-1, 1, cols)
    row_lines = token_mask.reshape(-1, 1, rows)
    line = lambda gain: gain[None, :]

    tall = math.gcd(rows, 16)
    shape = jax.ShapeDtypeStruct
    block = lambda *dims: pl.BlockSpec(dims, lambda n, *_: (n,) + (0,) * (len(dims) - 1))
    query, gate, state, total = pl.pallas_call(
        start_kernel,
        grid_spec=pltpu.PrefetchScalarGridSpec(
            num_scalar_prefetch=2,
            grid=(rows // tall,),
            in_specs=[
                block(tall, cols, width),
                pl.BlockSpec((1, 1, cols), lambda n, where, mask: (where[0], 0, 0)),
                whole((1, width)),
                whole((width, 4 * width)),
            ],
            out_specs=[
                block(tall, cols, width),
                block(tall, cols, width),
                block(tall, depth, width),
                block(tall, width),
            ],
        ),
        out_shape=[
            shape((rows, cols, width), BF16),
            shape((rows, cols, width), BF16),
            shape((rows, depth, width), BF16),
            shape((rows, width), BF16),
        ],
        compiler_params=params(),
        cost_estimate=cost(rows * cols, 6 * width * width),
        name="start",
    )(where, token_mask, pair, col_lines, line(start_gain), start_in)

    swap = [(n, lax.axis_size("row") - 1 - n) for n in range(lax.axis_size("row"))]
    state_b = lax.ppermute(state, "row", swap)
    total_b = lax.ppermute(total, "row", swap)

    wide = 16
    broad = math.gcd(rows, 16)
    steps = rows // broad
    chunks = column_chunks(cols, slots)
    extra_slabs = [pl.cdiv(size // slots, depth) for _, size in chunks]
    rooms = [slots * depth * more for more in extra_slabs]
    slabs = [
        (slots // 2, size // slots + more, depth, width)
        for (_, size), more in zip(chunks, extra_slabs)
    ]

    column = lambda n: pl.BlockSpec(
        (width, width), lambda *_: (0, n), pipeline_mode=pl.Buffered(1)
    )

    def middle(part, update, gain):
        offset, chunk = chunks[part]
        span = chunk // 2
        low = lambda n: jnp.minimum(n, steps - 1)
        high = lambda n: jnp.maximum(n - steps, 0)
        tile = pl.BlockSpec((broad, chunk, width), lambda n, *_: (low(n), offset // chunk, 0))
        by_col = lambda *dims: pl.BlockSpec(dims, lambda n, *_: (high(n), 0, 0))
        extra = [] if update is None else [update]
        return pl.pallas_call(
            functools.partial(middle_kernel, steps, offset),
            grid_spec=pltpu.PrefetchScalarGridSpec(
                num_scalar_prefetch=2,
                grid=(steps + chunk // span,),
                in_specs=[
                    *[pl.BlockSpec(memory_space=pl.ANY)] * 5,
                    whole((rows, width)),
                    whole((rows, width)),
                    pl.BlockSpec((1, 1, rows), lambda n, where, mask: (where[1], 0, 0)),
                    whole((1, width)),
                    whole((width, width)),
                    whole((1, width)),
                    column(1),
                    column(2),
                ]
                + [pl.BlockSpec(memory_space=pl.ANY)] * len(extra),
                out_specs=[
                    tile,
                    by_col(span, rows, width),
                    *[pl.BlockSpec(slabs[part], lambda *_: (0, 0, 0, 0))] * 2,
                ],
                scratch_shapes=[
                    pltpu.VMEM((rows * chunk, width), F32),
                    pltpu.VMEM((rooms[part], width), F32),
                    pltpu.VMEM((2 * width, width), BF16),
                    pltpu.VMEM((2, *slabs[part]), BF16),
                    *[pltpu.VMEM((rows, chunk, width), BF16)] * 3,
                    *[pltpu.VMEM((rows, depth, width), BF16)] * 2,
                    pltpu.SemaphoreType.DMA((steps, 5)),
                ],
            ),
            out_shape=[
                shape((rows, cols, width), BF16),
                shape((chunk, rows, width), BF16),
                *[shape(slabs[part], BF16)] * 2,
            ],
            input_output_aliases={15: 0} if extra else {},
            compiler_params=params(),
            cost_estimate=cost(rows * chunk, 7 * width * width),
            name="middle",
        )(
            where,
            token_mask,
            pair,
            query,
            gate,
            state,
            state_b,
            total,
            total_b,
            row_lines,
            line(start_head_gain),
            start_out,
            gain,
            end_in,
            end_in,
            *extra,
        )

    def queries(normed):
        chunk = normed.shape[0]
        span = chunk // 2
        return pl.pallas_call(
            query_kernel,
            grid=(chunk // span,),
            in_specs=[block(span, rows, width), column(0), column(3)],
            out_specs=[block(span, rows, width)] * 2,
            out_shape=[shape((chunk, rows, width), BF16)] * 2,
            compiler_params=params(),
            cost_estimate=cost(rows * chunk, 2 * width * width),
            name="queries",
        )(normed, end_in, end_in)

    def end(part, update_start, parts, outs, gain):
        offset, chunk = chunks[part]
        tile = pl.BlockSpec((rows, wide, width), lambda n, *_: (0, offset // wide + n, 0))
        return pl.pallas_call(
            end_kernel,
            grid_spec=pltpu.PrefetchScalarGridSpec(
                num_scalar_prefetch=1,
                grid=(chunk // wide,),
                in_specs=[
                    tile,
                    tile,
                    block(wide, rows, width),
                    block(wide, rows, width),
                    whole(slabs[part]),
                    whole(slabs[part]),
                    whole((1, width)),
                    whole((width, width)),
                    whole((1, width)),
                    whole((width, 2 * hidden)),
                    whole((hidden, width)),
                ]
                + [pl.BlockSpec(memory_space=pl.ANY)] * len(outs),
                out_specs=[tile, tile],
                scratch_shapes=[
                    pltpu.VMEM((rows * wide, width), F32),
                    pltpu.VMEM((rooms[part], width), F32),
                    pltpu.VMEM((2 * width, width), BF16),
                    pltpu.VMEM((2, *slabs[part]), BF16),
                ],
            ),
            out_shape=[shape((rows, cols, width), BF16)] * 2,
            input_output_aliases={12: 0, 13: 1} if outs else {},
            compiler_params=params(),
            cost_estimate=cost(rows * chunk, 2 * width * width + 3 * width * hidden),
            name="end",
        )(
            where,
            pair,
            update_start,
            *parts,
            line(end_head_gain),
            end_out,
            gain,
            trans_in,
            trans_out,
            *outs,
        )

    sums = []
    latest = []

    def advance(done):
        live = [n for n, (_, other) in enumerate(latest) if other is not None]
        if not live:
            return done, []
        done, *others = lax.optimization_barrier((done, *(latest[n][1] for n in live)))
        for n, other in zip(live, others):
            latest[n] = sums[n].send(other)
        return done, [*others, *jax.tree.leaves([latest[n][0] for n in live])]

    def after(value, behind):
        return lax.optimization_barrier((value, *behind))[0] if behind else value

    update_start = None
    outs = ()
    held = []
    behind = []
    for part in range(len(chunks)):
        update_start, normed, send, keep = middle(
            part, update_start, after(line(end_gain), behind)
        )
        held.append(normed)
        send, behind = advance(send)
        sums.append(column_sum(send, keep))
        latest.append(next(sums[-1]))
        behind.append(latest[-1][0])
    waiting = list(range(len(chunks)))
    for part in range(len(chunks)):
        while latest[part][1] is not None:
            batch = waiting
            waiting = waiting[len(batch) :]
            for n in batch:
                held[n] = queries(after(held[n], behind))
            if batch:
                first, behind = advance(held[batch[-1]][0])
                held[batch[-1]] = (first, held[batch[-1]][1])
            else:
                _, behind = advance(line(trans_gain))
        for n in waiting:
            held[n] = queries(held[n])
        waiting = []
        gain = after(line(trans_gain), behind)
        outs = end(part, update_start, (*held[part], *latest[part][0]), outs, gain)
        first, behind = advance(outs[0])
        outs = (first, outs[1])
    return (update_start, outs[0], outs[1])


def solution(mesh):
    pair_spec = P(("groups", "col"), "row", None)
    return jax.shard_map(
        shards,
        mesh=mesh,
        in_specs=(pair_spec, P("groups")) + (P(),) * 11,
        out_specs=(pair_spec,) * 3,
        check_vma=False,
    )
```

```python
import functools
import math

import jax
import jax.numpy as jnp
from jax import lax
from jax.experimental import pallas as pl
from jax.experimental.pallas import tpu as pltpu
from jax.sharding import PartitionSpec as P

HEADS = 4
EPSILON = 1e-05
BF16 = jnp.bfloat16
F32 = jnp.float32
NT = (((1,), (1,)), ((), ()))


def params():
    return pltpu.CompilerParams(
        dimension_semantics=("arbitrary",),
        vmem_limit_bytes=56 * 1024 * 1024,
    )


def cost(pairs, products):
    return pl.CostEstimate(
        flops=16 * pairs * products, transcendentals=0, bytes_accessed=64 * pairs
    )


def square_block(width, centering):
    row = lax.broadcasted_iota(jnp.int32, (2 * width, 2 * width), 0)
    lane = lax.broadcasted_iota(jnp.int32, (2 * width, 2 * width), 1)
    if centering:
        block = jnp.where(row == lane, 1.0 - 1.0 / width, -1.0 / width)
    else:
        block = jnp.ones((2 * width, 2 * width), F32)
    return jnp.where(row // width == lane // width, block, 0.0).astype(BF16)


def paired(values, block):
    half, width = values.shape[0] // 2, values.shape[1]
    sides = jnp.concatenate([values[:half], values[half:]], axis=1)
    both = jnp.dot(sides, block, preferred_element_type=F32)
    return jnp.concatenate([both[:, :width], both[:, width:]], axis=0)


def summed_center(one, two):
    width = one.shape[1]
    center = square_block(width, True)[:width, :width]
    return jnp.dot(
        jnp.concatenate([one, two], axis=1),
        jnp.concatenate([center, center], axis=0),
        preferred_element_type=F32,
    )


def norm(centered, gain, by_product=True):
    width = centered.shape[-1]
    if by_product:
        square = paired((centered * centered).astype(BF16), square_block(width, False))
    else:
        square = jnp.sum(centered * centered, axis=-1, keepdims=True)
    return (centered * lax.rsqrt(square + EPSILON * width) * (gain * math.sqrt(width))).astype(BF16)


def feature(values):
    values = values.astype(BF16)
    return jnp.where(values > 0, values + 1.0, jnp.exp(values))


def gating(halves):
    return jnp.tanh(halves.astype(BF16)) + 1.0


def key_state(keys, values, mask_row):
    width = keys.shape[-1]
    depth = width // HEADS
    turned = values.T * mask_row
    ones = jnp.broadcast_to(mask_row, (16, mask_row.shape[-1]))
    full = jnp.dot(jnp.concatenate([turned, ones], axis=0), keys, preferred_element_type=F32)
    lane_head = lax.broadcasted_iota(jnp.int32, (depth, width), 1) // depth
    packed = jnp.zeros((depth, width), F32)
    for head in range(HEADS):
        packed = jnp.where(lane_head == head, full[head * depth : (head + 1) * depth], packed)
    return packed, full[width : width + 1]


def key_states(keys, values, mask_row, block, inner):
    pick = lambda part, n: part[n * inner : (n + 1) * inner].astype(BF16)
    return [key_state(pick(keys, n), pick(values, n), mask_row) for n in range(block)]


def fill_block_mask(block_mask):
    double, width = block_mask.shape
    depth = width // HEADS
    row_head = lax.broadcasted_iota(jnp.int32, (double, width), 0) // depth % HEADS
    lane_head = lax.broadcasted_iota(jnp.int32, (double, width), 1) // depth
    block_mask[...] = jnp.where(row_head == lane_head, 1.0, 0.0).astype(BF16)


def attend(queries, packed, totals, block_mask):
    width = queries.shape[-1]
    spread = jnp.concatenate([packed] * HEADS, axis=0)
    right = jnp.concatenate([spread, jnp.broadcast_to(totals, (width, width))], axis=0)
    both = lax.dot_general(queries, right * block_mask, NT, preferred_element_type=F32)
    return both[:, :width] / jnp.maximum(both[:, width:], 1.0)


def head_norm(attended, gain, gate):
    width = attended.shape[-1]
    square = jnp.sum(attended * attended, axis=-1, keepdims=True)
    scaled = attended * lax.rsqrt(square + EPSILON * width) * (gain * (0.5 * math.sqrt(width)))
    return (scaled * gate).astype(BF16)


def start_kernel(where, mask, pair, line, gain, w_in, query_out, gate_out, state_out, total_out):
    rows, cols, width = pair.shape
    base = where[1] * (rows * pl.num_programs(0)) + pl.program_id(0) * rows
    centered = paired(pair[...].reshape(rows * cols, width), square_block(width, True))
    x = norm(centered, gain[...], False)
    w = w_in[...]
    w = jnp.concatenate([w[:, : 3 * width], w[:, 3 * width :] * 0.5], axis=1)
    project = jnp.dot(x, w, preferred_element_type=F32)
    fold = lambda part: part.reshape(rows, cols, width)
    query_out[...] = fold(feature(project[:, :width]))
    gate_out[...] = fold(gating(project[:, 3 * width :]))
    keys = feature(project[:, width : 2 * width])
    values = project[:, 2 * width : 3 * width]
    col_mask = line[0].astype(F32).astype(BF16)
    lines = []
    for r, (packed, totals) in enumerate(key_states(keys, values, col_mask, rows, cols)):
        valid = mask[base + r].astype(F32)
        state_out[r] = (packed * valid).astype(BF16)
        lines.append(totals * valid)
    total_out[...] = jnp.concatenate(lines, axis=0).astype(BF16)


def middle_kernel(
    steps,
    offset,
    where,
    mask,
    pair,
    query,
    gate,
    state_a,
    state_b,
    total_a,
    total_b,
    line,
    head_gain,
    w_out,
    gain,
    w_key,
    w_value,
    *rest,
):
    update_out, normed_out, send_out, keep_out, anchor, held, block_mask, staged = rest[-14:-6]
    *landed, arrived = rest[-6:]
    block_rows, cols, width = update_out.shape
    block_cols, rows, _ = normed_out.shape
    _, half, _, depth, _ = staged.shape
    share, room = cols // (2 * half), held.shape[0] // (2 * half)
    step = pl.program_id(0)
    side = where[1] % 2
    spot = lambda slot: (1 - jnp.abs(slot // half - side), slot % half)

    def fetches(index):
        some = pl.ds(index * block_rows, block_rows)
        own = pl.ds(offset, cols)
        sources = [n.at[some, own] for n in (query, gate, pair)]
        sources += [n.at[some] for n in (state_a, state_b)]
        return [
            pltpu.make_async_copy(source, target.at[some], arrived.at[index, n])
            for n, (source, target) in enumerate(zip(sources, landed))
        ]

    @pl.when(step == 0)
    def _():
        for index in range(steps):
            for fetch in fetches(index):
                fetch.start()
        fill_block_mask(block_mask)
        held[...] = jnp.zeros_like(held)

    @pl.when(step < steps)
    def _():
        for fetch in fetches(step):
            fetch.wait()
        some = pl.ds(step * block_rows, block_rows)
        queries, gates, pairs = (n[some] for n in landed[:3])
        mine, others = (n[some].astype(F32) for n in landed[3:])
        both = (mine + others).astype(BF16)
        lines = (total_a[some].astype(F32) + total_b[some].astype(F32)).astype(BF16)
        attended = []
        for r in range(block_rows):
            attended.append(attend(queries[r], both[r], lines[r : r + 1], block_mask[...]))
        flat = (block_rows * cols, width)
        attended = jnp.concatenate(attended, axis=0)
        scaled = head_norm(attended, head_gain[...], gates.astype(F32).reshape(flat))
        update = jnp.dot(scaled, w_out[...], preferred_element_type=F32).astype(BF16)
        update_out[...] = update.reshape(block_rows, cols, width)
        centered = summed_center(pairs.reshape(flat), update)
        anchor[pl.ds(step * block_rows * cols, block_rows * cols), :] = centered

    @pl.when(step >= steps)
    def _():
        base = (step - steps) * block_cols
        centered = [anchor[pl.ds(base + c, rows, stride=cols), :] for c in range(block_cols)]
        x = norm(jnp.concatenate(centered, axis=0), gain[...], False)
        normed_out[...] = x.reshape(block_cols, rows, width)
        w = jnp.concatenate([w_key[...], w_value[...]], axis=1)
        project = jnp.dot(x, w, preferred_element_type=F32)
        keys, values = feature(project[:, :width]), project[:, width:]
        row_mask = line[0].astype(F32).astype(BF16)
        start = where[0] * (mask.shape[0] // where[2]) + offset
        for c, (packed, totals) in enumerate(
            key_states(keys, values, row_mask, block_cols, rows)
        ):
            place = base + c
            valid = mask[start + place].astype(F32)
            staged[*spot(place // share), place % share] = (packed * valid).astype(BF16)
            held[pl.ds(place // share * room + place % share, 1), :] = totals * valid

    @pl.when(step == pl.num_programs(0) - 1)
    def _():
        for slot in range(2 * half):
            for low in range(0, room, depth):
                lines = held[pl.ds(slot * room + low, depth), :].astype(BF16)
                staged[*spot(slot), share + low // depth] = lines
        send_out[...] = staged[0]
        keep_out[...] = staged[1]


def query_kernel(normed, w_query, w_gate, query_out, gate_out):
    cols, rows, width = normed.shape
    x = normed[...].astype(F32).reshape(cols * rows, width).astype(BF16)
    w = jnp.concatenate([w_query[...], w_gate[...] * 0.5], axis=1)
    project = jnp.dot(x, w, preferred_element_type=F32)
    fold = lambda part: part.astype(F32).reshape(cols, rows, width).astype(BF16)
    query_out[...] = fold(feature(project[:, :width]))
    gate_out[...] = fold(gating(project[:, width:]))


def end_kernel(
    where,
    pair,
    update_start,
    query,
    gate,
    mine,
    other,
    head_gain,
    w_out,
    gain,
    w_in,
    w_down,
    *rest,
):
    update_out, trans_out, turned, held, block_mask, state = rest[-6:]
    rows, block_cols, width = pair.shape
    hidden = w_down.shape[0]
    _, half, _, depth, _ = state.shape
    share = pl.num_programs(0) * block_cols // (2 * half)
    room = held.shape[0] // (2 * half)
    step = pl.program_id(0)

    @pl.when(step == 0)
    def _():
        fill_block_mask(block_mask)
        side = where[1] % 2
        state[side] = mine[...]
        state[1 - side] = other[...]
        for slot in range(2 * half):
            for low in range(0, room, depth):
                lines = state[slot // half, slot % half, share + low // depth].astype(F32)
                held[pl.ds(slot * room + low, depth), :] = lines

    attended = []
    for c in range(block_cols):
        place = step * block_cols + c
        slot = place // share
        packed = state[slot // half, slot % half, place % share]
        totals = held[pl.ds(slot * room + place % share, 1), :].astype(BF16)
        attended.append(attend(query[c], packed, totals, block_mask[...]))
    flat = (rows * block_cols, width)
    attended = jnp.concatenate(attended, axis=0)
    scaled = head_norm(attended, head_gain[...], gate[...].astype(F32).reshape(flat))
    update = jnp.dot(scaled, w_out[...], preferred_element_type=F32)
    for c in range(block_cols):
        turned[pl.ds(c, rows, stride=block_cols), :] = update[c * rows : (c + 1) * rows]
    update = turned[...].astype(BF16)
    update_out[...] = update.reshape(rows, block_cols, width)
    first = pair[...].astype(F32) + update_start[...].astype(F32)
    second = first.reshape(flat) + update.astype(F32)
    centered = second - jnp.sum(second, axis=-1, keepdims=True) * (1.0 / width)
    x = norm(centered, gain[...])
    w = w_in[...]
    w = jnp.concatenate([w[:, :hidden] * 0.5, w[:, hidden:]], axis=1)
    lifted = jnp.dot(x, w, preferred_element_type=F32).astype(BF16)
    half = lifted[:, :hidden]
    inner = half * (jnp.tanh(half) + 1.0) * lifted[:, hidden:]
    down = jnp.dot(inner, w_down[...], preferred_element_type=F32)
    trans_out[...] = down.reshape(rows, block_cols, width).astype(BF16)


def column_sum(send, keep):
    size = lax.axis_size("col")
    swap = lambda part, bit: lax.ppermute(part, "col", [(n, n ^ bit) for n in range(size)])
    add = lambda one, two: (one.astype(F32) + two.astype(F32)).astype(BF16)
    other = yield send, swap(send, 1)
    state = add(keep, other)
    for bit in [1 << n for n in range(1, size.bit_length() - 1)]:
        other = yield state, swap(state, bit)
        state = add(state, other)
    other = yield state, swap(state, 1)
    yield (state, other), None


def column_chunks(cols, slots):
    count = 4
    while count > 1 and (cols % count or cols // count % 16 or cols // count % slots):
        count -= 1
    return [(n * (cols // count), cols // count) for n in range(count)]


def whole(shape):
    return pl.BlockSpec(shape, lambda *_: (0,) * len(shape), pipeline_mode=pl.Buffered(1))


def shards(
    pair,
    token_mask,
    start_gain,
    start_head_gain,
    start_in,
    start_out,
    end_gain,
    end_head_gain,
    end_in,
    end_out,
    trans_gain,
    trans_in,
    trans_out,
):
    rows, cols, width = pair.shape
    depth = width // HEADS
    hidden = trans_out.shape[0]
    slots = 2
    where = jnp.stack(
        [lax.axis_index("row"), lax.axis_index("col"), jnp.int32(lax.axis_size("row"))]
    ).astype(jnp.int32)
    col_lines = token_mask.reshape(-1, 1, cols)
    row_lines = token_mask.reshape(-1, 1, rows)
    line = lambda gain: gain[None, :]

    tall = math.gcd(rows, 16)
    shape = jax.ShapeDtypeStruct
    block = lambda *dims: pl.BlockSpec(dims, lambda n, *_: (n,) + (0,) * (len(dims) - 1))
    query, gate, state, total = pl.pallas_call(
        start_kernel,
        grid_spec=pltpu.PrefetchScalarGridSpec(
            num_scalar_prefetch=2,
            grid=(rows // tall,),
            in_specs=[
                block(tall, cols, width),
                pl.BlockSpec((1, 1, cols), lambda n, where, mask: (where[0], 0, 0)),
                whole((1, width)),
                whole((width, 4 * width)),
            ],
            out_specs=[
                block(tall, cols, width),
                block(tall, cols, width),
                block(tall, depth, width),
                block(tall, width),
            ],
        ),
        out_shape=[
            shape((rows, cols, width), BF16),
            shape((rows, cols, width), BF16),
            shape((rows, depth, width), BF16),
            shape((rows, width), BF16),
        ],
        compiler_params=params(),
        cost_estimate=cost(rows * cols, 6 * width * width),
        name="start",
    )(where, token_mask, pair, col_lines, line(start_gain), start_in)

    swap = [(n, lax.axis_size("row") - 1 - n) for n in range(lax.axis_size("row"))]
    state_b = lax.ppermute(state, "row", swap)
    total_b = lax.ppermute(total, "row", swap)

    wide = 16
    broad = math.gcd(rows, 16)
    steps = rows // broad
    chunks = column_chunks(cols, slots)
    extra_slabs = [pl.cdiv(size // slots, depth) for _, size in chunks]
    rooms = [slots * depth * more for more in extra_slabs]
    slabs = [
        (slots // 2, size // slots + more, depth, width)
        for (_, size), more in zip(chunks, extra_slabs)
    ]

    column = lambda n: pl.BlockSpec(
        (width, width), lambda *_: (0, n), pipeline_mode=pl.Buffered(1)
    )

    def middle(part, update, gain):
        offset, chunk = chunks[part]
        span = chunk // 2
        low = lambda n: jnp.minimum(n, steps - 1)
        high = lambda n: jnp.maximum(n - steps, 0)
        tile = pl.BlockSpec((broad, chunk, width), lambda n, *_: (low(n), offset // chunk, 0))
        by_col = lambda *dims: pl.BlockSpec(dims, lambda n, *_: (high(n), 0, 0))
        extra = [] if update is None else [update]
        return pl.pallas_call(
            functools.partial(middle_kernel, steps, offset),
            grid_spec=pltpu.PrefetchScalarGridSpec(
                num_scalar_prefetch=2,
                grid=(steps + chunk // span,),
                in_specs=[
                    *[pl.BlockSpec(memory_space=pl.ANY)] * 5,
                    whole((rows, width)),
                    whole((rows, width)),
                    pl.BlockSpec((1, 1, rows), lambda n, where, mask: (where[1], 0, 0)),
                    whole((1, width)),
                    whole((width, width)),
                    whole((1, width)),
                    column(1),
                    column(2),
                ]
                + [pl.BlockSpec(memory_space=pl.ANY)] * len(extra),
                out_specs=[
                    tile,
                    by_col(span, rows, width),
                    *[pl.BlockSpec(slabs[part], lambda *_: (0, 0, 0, 0))] * 2,
                ],
                scratch_shapes=[
                    pltpu.VMEM((rows * chunk, width), F32),
                    pltpu.VMEM((rooms[part], width), F32),
                    pltpu.VMEM((2 * width, width), BF16),
                    pltpu.VMEM((2, *slabs[part]), BF16),
                    *[pltpu.VMEM((rows, chunk, width), BF16)] * 3,
                    *[pltpu.VMEM((rows, depth, width), BF16)] * 2,
                    pltpu.SemaphoreType.DMA((steps, 5)),
                ],
            ),
            out_shape=[
                shape((rows, cols, width), BF16),
                shape((chunk, rows, width), BF16),
                *[shape(slabs[part], BF16)] * 2,
            ],
            input_output_aliases={15: 0} if extra else {},
            compiler_params=params(),
            cost_estimate=cost(rows * chunk, 7 * width * width),
            name="middle",
        )(
            where,
            token_mask,
            pair,
            query,
            gate,
            state,
            state_b,
            total,
            total_b,
            row_lines,
            line(start_head_gain),
            start_out,
            gain,
            end_in,
            end_in,
            *extra,
        )

    def queries(normed):
        chunk = normed.shape[0]
        span = chunk // 2
        return pl.pallas_call(
            query_kernel,
            grid=(chunk // span,),
            in_specs=[block(span, rows, width), column(0), column(3)],
            out_specs=[block(span, rows, width)] * 2,
            out_shape=[shape((chunk, rows, width), BF16)] * 2,
            compiler_params=params(),
            cost_estimate=cost(rows * chunk, 2 * width * width),
            name="queries",
        )(normed, end_in, end_in)

    def end(part, update_start, parts, outs, gain):
        offset, chunk = chunks[part]
        tile = pl.BlockSpec((rows, wide, width), lambda n, *_: (0, offset // wide + n, 0))
        return pl.pallas_call(
            end_kernel,
            grid_spec=pltpu.PrefetchScalarGridSpec(
                num_scalar_prefetch=1,
                grid=(chunk // wide,),
                in_specs=[
                    tile,
                    tile,
                    block(wide, rows, width),
                    block(wide, rows, width),
                    whole(slabs[part]),
                    whole(slabs[part]),
                    whole((1, width)),
                    whole((width, width)),
                    whole((1, width)),
                    whole((width, 2 * hidden)),
                    whole((hidden, width)),
                ]
                + [pl.BlockSpec(memory_space=pl.ANY)] * len(outs),
                out_specs=[tile, tile],
                scratch_shapes=[
                    pltpu.VMEM((rows * wide, width), F32),
                    pltpu.VMEM((rooms[part], width), F32),
                    pltpu.VMEM((2 * width, width), BF16),
                    pltpu.VMEM((2, *slabs[part]), BF16),
                ],
            ),
            out_shape=[shape((rows, cols, width), BF16)] * 2,
            input_output_aliases={12: 0, 13: 1} if outs else {},
            compiler_params=params(),
            cost_estimate=cost(rows * chunk, 2 * width * width + 3 * width * hidden),
            name="end",
        )(
            where,
            pair,
            update_start,
            *parts,
            line(end_head_gain),
            end_out,
            gain,
            trans_in,
            trans_out,
            *outs,
        )

    sums = []
    latest = []

    def advance(done):
        live = [n for n, (_, other) in enumerate(latest) if other is not None]
        if not live:
            return done, []
        done, *others = lax.optimization_barrier((done, *(latest[n][1] for n in live)))
        for n, other in zip(live, others):
            latest[n] = sums[n].send(other)
        return done, [*others, *jax.tree.leaves([latest[n][0] for n in live])]

    def after(value, behind):
        return lax.optimization_barrier((value, *behind))[0] if behind else value

    update_start = None
    outs = ()
    held = []
    behind = []
    for part in range(len(chunks)):
        update_start, normed, send, keep = middle(
            part, update_start, after(line(end_gain), behind)
        )
        held.append(normed)
        if part > 0 and part == len(chunks) - 1:
            held[0] = queries(after(held[0], [send]))
            first, behind = advance(held[0][0])
            held[0] = (first, held[0][1])
        else:
            send, behind = advance(send)
        sums.append(column_sum(send, keep))
        latest.append(next(sums[-1]))
        behind.append(latest[-1][0])
    waiting = list(range(1 if len(chunks) > 1 else 0, len(chunks)))
    for part in range(len(chunks)):
        while latest[part][1] is not None:
            batch = waiting
            waiting = waiting[len(batch) :]
            for n in batch:
                held[n] = queries(after(held[n], behind))
            if batch:
                first, behind = advance(held[batch[-1]][0])
                held[batch[-1]] = (first, held[batch[-1]][1])
            else:
                _, behind = advance(line(trans_gain))
        for n in waiting:
            held[n] = queries(held[n])
        waiting = []
        gain = after(line(trans_gain), behind)
        outs = end(part, update_start, (*held[part], *latest[part][0]), outs, gain)
        first, behind = advance(outs[0])
        outs = (first, outs[1])
    return (update_start, outs[0], outs[1])


def solution(mesh):
    pair_spec = P(("groups", "col"), "row", None)
    return jax.shard_map(
        shards,
        mesh=mesh,
        in_specs=(pair_spec, P("groups")) + (P(),) * 11,
        out_specs=(pair_spec,) * 3,
        check_vma=False,
    )
```

```python
import functools
import math

import jax
import jax.numpy as jnp
from jax import lax
from jax.experimental import pallas as pl
from jax.experimental.pallas import tpu as pltpu
from jax.sharding import PartitionSpec as P

HEADS = 4
EPSILON = 1e-05
BF16 = jnp.bfloat16
F32 = jnp.float32
NT = (((1,), (1,)), ((), ()))


def params():
    return pltpu.CompilerParams(
        dimension_semantics=("arbitrary",),
        vmem_limit_bytes=56 * 1024 * 1024,
    )


def cost(pairs, products):
    return pl.CostEstimate(
        flops=16 * pairs * products, transcendentals=0, bytes_accessed=64 * pairs
    )


def square_block(width, centering):
    row = lax.broadcasted_iota(jnp.int32, (2 * width, 2 * width), 0)
    lane = lax.broadcasted_iota(jnp.int32, (2 * width, 2 * width), 1)
    if centering:
        block = jnp.where(row == lane, 1.0 - 1.0 / width, -1.0 / width)
    else:
        block = jnp.ones((2 * width, 2 * width), F32)
    return jnp.where(row // width == lane // width, block, 0.0).astype(BF16)


def paired(values, block):
    half, width = values.shape[0] // 2, values.shape[1]
    sides = jnp.concatenate([values[:half], values[half:]], axis=1)
    both = jnp.dot(sides, block, preferred_element_type=F32)
    return jnp.concatenate([both[:, :width], both[:, width:]], axis=0)


def summed_center(one, two):
    width = one.shape[1]
    center = square_block(width, True)[:width, :width]
    return jnp.dot(
        jnp.concatenate([one, two], axis=1),
        jnp.concatenate([center, center], axis=0),
        preferred_element_type=F32,
    )


def norm(centered, gain, by_product=True):
    width = centered.shape[-1]
    if by_product:
        square = paired((centered * centered).astype(BF16), square_block(width, False))
    else:
        square = jnp.sum(centered * centered, axis=-1, keepdims=True)
    return (centered * lax.rsqrt(square + EPSILON * width) * (gain * math.sqrt(width))).astype(BF16)


def feature(values):
    values = values.astype(BF16)
    return jnp.where(values > 0, values + 1.0, jnp.exp(values))


def gating(halves):
    return jnp.tanh(halves.astype(BF16)) + 1.0


def key_state(keys, values, mask_row):
    width = keys.shape[-1]
    depth = width // HEADS
    turned = values.T * mask_row
    ones = jnp.broadcast_to(mask_row, (16, mask_row.shape[-1]))
    full = jnp.dot(jnp.concatenate([turned, ones], axis=0), keys, preferred_element_type=F32)
    lane_head = lax.broadcasted_iota(jnp.int32, (depth, width), 1) // depth
    packed = jnp.zeros((depth, width), F32)
    for head in range(HEADS):
        packed = jnp.where(lane_head == head, full[head * depth : (head + 1) * depth], packed)
    return packed, full[width : width + 1]


def key_states(keys, values, mask_row, block, inner):
    pick = lambda part, n: part[n * inner : (n + 1) * inner].astype(BF16)
    return [key_state(pick(keys, n), pick(values, n), mask_row) for n in range(block)]


def fill_block_mask(block_mask):
    double, width = block_mask.shape
    depth = width // HEADS
    row_head = lax.broadcasted_iota(jnp.int32, (double, width), 0) // depth % HEADS
    lane_head = lax.broadcasted_iota(jnp.int32, (double, width), 1) // depth
    block_mask[...] = jnp.where(row_head == lane_head, 1.0, 0.0).astype(BF16)


def attend(queries, packed, totals, block_mask):
    width = queries.shape[-1]
    spread = jnp.concatenate([packed] * HEADS, axis=0)
    right = jnp.concatenate([spread, jnp.broadcast_to(totals, (width, width))], axis=0)
    both = lax.dot_general(queries, right * block_mask, NT, preferred_element_type=F32)
    return both[:, :width] / jnp.maximum(both[:, width:], 1.0)


def head_norm(attended, gain, gate):
    width = attended.shape[-1]
    square = jnp.sum(attended * attended, axis=-1, keepdims=True)
    scaled = attended * lax.rsqrt(square + EPSILON * width) * (gain * (0.5 * math.sqrt(width)))
    return (scaled * gate).astype(BF16)


def mask_line(mask, index, size):
    tokens = mask.shape[0]
    spread = mask[...].astype(F32).reshape(1, tokens)
    row = jnp.zeros((1, size), F32)
    for n in range(tokens // size):
        row = jnp.where(index == n, spread[:, n * size : (n + 1) * size], row)
    return row.astype(BF16)


def start_kernel(where, mask, pair, line, gain, w_in, query_out, gate_out, state_out, total_out):
    rows, cols, width = pair.shape
    base = where[1] * (rows * pl.num_programs(0)) + pl.program_id(0) * rows
    centered = paired(pair[...].reshape(rows * cols, width), square_block(width, True))
    x = norm(centered, gain[...], False)
    w = w_in[...]
    w = jnp.concatenate([w[:, : 3 * width], w[:, 3 * width :] * 0.5], axis=1)
    project = jnp.dot(x, w, preferred_element_type=F32)
    fold = lambda part: part.reshape(rows, cols, width)
    query_out[...] = fold(feature(project[:, :width]))
    gate_out[...] = fold(gating(project[:, 3 * width :]))
    keys = feature(project[:, width : 2 * width])
    values = project[:, 2 * width : 3 * width]
    col_mask = mask_line(line, where[0], cols)
    lines = []
    for r, (packed, totals) in enumerate(key_states(keys, values, col_mask, rows, cols)):
        valid = mask[base + r].astype(F32)
        state_out[r] = (packed * valid).astype(BF16)
        lines.append(totals * valid)
    total_out[...] = jnp.concatenate(lines, axis=0).astype(BF16)


def middle_kernel(
    steps,
    offset,
    where,
    mask,
    pair,
    query,
    gate,
    state_a,
    state_b,
    total_a,
    total_b,
    line,
    head_gain,
    w_out,
    gain,
    w_key,
    w_value,
    *rest,
):
    update_out, normed_out, send_out, keep_out, anchor, held, block_mask, staged = rest[-14:-6]
    *landed, arrived = rest[-6:]
    block_rows, cols, width = update_out.shape
    block_cols, rows, _ = normed_out.shape
    _, half, _, depth, _ = staged.shape
    share, room = cols // (2 * half), held.shape[0] // (2 * half)
    step = pl.program_id(0)
    side = where[1] % 2
    spot = lambda slot: (1 - jnp.abs(slot // half - side), slot % half)

    def fetches(index):
        some = pl.ds(index * block_rows, block_rows)
        own = pl.ds(offset, cols)
        sources = [n.at[some, own] for n in (query, gate, pair)]
        sources += [n.at[some] for n in (state_a, state_b)]
        return [
            pltpu.make_async_copy(source, target.at[some], arrived.at[index, n])
            for n, (source, target) in enumerate(zip(sources, landed))
        ]

    @pl.when(step == 0)
    def _():
        for index in range(steps):
            for fetch in fetches(index):
                fetch.start()
        fill_block_mask(block_mask)
        held[...] = jnp.zeros_like(held)

    @pl.when(step < steps)
    def _():
        for fetch in fetches(step):
            fetch.wait()
        some = pl.ds(step * block_rows, block_rows)
        queries, gates, pairs = (n[some] for n in landed[:3])
        mine, others = (n[some].astype(F32) for n in landed[3:])
        both = (mine + others).astype(BF16)
        lines = (total_a[some].astype(F32) + total_b[some].astype(F32)).astype(BF16)
        attended = []
        for r in range(block_rows):
            attended.append(attend(queries[r], both[r], lines[r : r + 1], block_mask[...]))
        flat = (block_rows * cols, width)
        attended = jnp.concatenate(attended, axis=0)
        scaled = head_norm(attended, head_gain[...], gates.astype(F32).reshape(flat))
        update = jnp.dot(scaled, w_out[...], preferred_element_type=F32).astype(BF16)
        update_out[...] = update.reshape(block_rows, cols, width)
        centered = summed_center(pairs.reshape(flat), update)
        anchor[pl.ds(step * block_rows * cols, block_rows * cols), :] = centered

    @pl.when(step >= steps)
    def _():
        base = (step - steps) * block_cols
        centered = [anchor[pl.ds(base + c, rows, stride=cols), :] for c in range(block_cols)]
        x = norm(jnp.concatenate(centered, axis=0), gain[...], False)
        normed_out[...] = x.reshape(block_cols, rows, width)
        w = jnp.concatenate([w_key[...], w_value[...]], axis=1)
        project = jnp.dot(x, w, preferred_element_type=F32)
        keys, values = feature(project[:, :width]), project[:, width:]
        row_mask = mask_line(line, where[1], rows)
        start = where[0] * (mask.shape[0] // where[2]) + offset
        for c, (packed, totals) in enumerate(
            key_states(keys, values, row_mask, block_cols, rows)
        ):
            place = base + c
            valid = mask[start + place].astype(F32)
            staged[*spot(place // share), place % share] = (packed * valid).astype(BF16)
            held[pl.ds(place // share * room + place % share, 1), :] = totals * valid

    @pl.when(step == pl.num_programs(0) - 1)
    def _():
        for slot in range(2 * half):
            for low in range(0, room, depth):
                lines = held[pl.ds(slot * room + low, depth), :].astype(BF16)
                staged[*spot(slot), share + low // depth] = lines
        send_out[...] = staged[0]
        keep_out[...] = staged[1]


def query_kernel(normed, w_query, w_gate, query_out, gate_out):
    cols, rows, width = normed.shape
    x = normed[...].astype(F32).reshape(cols * rows, width).astype(BF16)
    w = jnp.concatenate([w_query[...], w_gate[...] * 0.5], axis=1)
    project = jnp.dot(x, w, preferred_element_type=F32)
    fold = lambda part: part.astype(F32).reshape(cols, rows, width).astype(BF16)
    query_out[...] = fold(feature(project[:, :width]))
    gate_out[...] = fold(gating(project[:, width:]))


def end_kernel(
    where,
    pair,
    update_start,
    query,
    gate,
    mine,
    other,
    head_gain,
    w_out,
    gain,
    w_in,
    w_down,
    *rest,
):
    update_out, trans_out, turned, held, block_mask, state = rest[-6:]
    rows, block_cols, width = pair.shape
    hidden = w_down.shape[0]
    _, half, _, depth, _ = state.shape
    share = pl.num_programs(0) * block_cols // (2 * half)
    room = held.shape[0] // (2 * half)
    step = pl.program_id(0)

    @pl.when(step == 0)
    def _():
        fill_block_mask(block_mask)
        side = where[1] % 2
        state[side] = mine[...]
        state[1 - side] = other[...]
        for slot in range(2 * half):
            for low in range(0, room, depth):
                lines = state[slot // half, slot % half, share + low // depth].astype(F32)
                held[pl.ds(slot * room + low, depth), :] = lines

    attended = []
    for c in range(block_cols):
        place = step * block_cols + c
        slot = place // share
        packed = state[slot // half, slot % half, place % share]
        totals = held[pl.ds(slot * room + place % share, 1), :].astype(BF16)
        attended.append(attend(query[c], packed, totals, block_mask[...]))
    flat = (rows * block_cols, width)
    attended = jnp.concatenate(attended, axis=0)
    scaled = head_norm(attended, head_gain[...], gate[...].astype(F32).reshape(flat))
    update = jnp.dot(scaled, w_out[...], preferred_element_type=F32)
    for c in range(block_cols):
        turned[pl.ds(c, rows, stride=block_cols), :] = update[c * rows : (c + 1) * rows]
    update = turned[...].astype(BF16)
    update_out[...] = update.reshape(rows, block_cols, width)
    first = pair[...].astype(F32) + update_start[...].astype(F32)
    second = first.reshape(flat) + update.astype(F32)
    centered = second - jnp.sum(second, axis=-1, keepdims=True) * (1.0 / width)
    x = norm(centered, gain[...])
    w = w_in[...]
    w = jnp.concatenate([w[:, :hidden] * 0.5, w[:, hidden:]], axis=1)
    lifted = jnp.dot(x, w, preferred_element_type=F32).astype(BF16)
    half = lifted[:, :hidden]
    inner = half * (jnp.tanh(half) + 1.0) * lifted[:, hidden:]
    down = jnp.dot(inner, w_down[...], preferred_element_type=F32)
    trans_out[...] = down.reshape(rows, block_cols, width).astype(BF16)


def column_sum(send, keep):
    size = lax.axis_size("col")
    swap = lambda part, bit: lax.ppermute(part, "col", [(n, n ^ bit) for n in range(size)])
    add = lambda one, two: (one.astype(F32) + two.astype(F32)).astype(BF16)
    other = yield send, swap(send, 1)
    state = add(keep, other)
    for bit in [1 << n for n in range(1, size.bit_length() - 1)]:
        other = yield state, swap(state, bit)
        state = add(state, other)
    other = yield state, swap(state, 1)
    yield (state, other), None


def column_chunks(cols, slots):
    count = 4
    while count > 1 and (cols % count or cols // count % 16 or cols // count % slots):
        count -= 1
    return [(n * (cols // count), cols // count) for n in range(count)]


def whole(shape):
    return pl.BlockSpec(shape, lambda *_: (0,) * len(shape), pipeline_mode=pl.Buffered(1))


def shards(
    pair,
    token_mask,
    start_gain,
    start_head_gain,
    start_in,
    start_out,
    end_gain,
    end_head_gain,
    end_in,
    end_out,
    trans_gain,
    trans_in,
    trans_out,
):
    rows, cols, width = pair.shape
    depth = width // HEADS
    hidden = trans_out.shape[0]
    slots = 2
    where = jnp.stack(
        [lax.axis_index("row"), lax.axis_index("col"), jnp.int32(lax.axis_size("row"))]
    ).astype(jnp.int32)
    line = lambda gain: gain[None, :]

    tall = math.gcd(rows, 16)
    shape = jax.ShapeDtypeStruct
    block = lambda *dims: pl.BlockSpec(dims, lambda n, *_: (n,) + (0,) * (len(dims) - 1))
    query, gate, state, total = pl.pallas_call(
        start_kernel,
        grid_spec=pltpu.PrefetchScalarGridSpec(
            num_scalar_prefetch=2,
            grid=(rows // tall,),
            in_specs=[
                block(tall, cols, width),
                whole(token_mask.shape),
                whole((1, width)),
                whole((width, 4 * width)),
            ],
            out_specs=[
                block(tall, cols, width),
                block(tall, cols, width),
                block(tall, depth, width),
                block(tall, width),
            ],
        ),
        out_shape=[
            shape((rows, cols, width), BF16),
            shape((rows, cols, width), BF16),
            shape((rows, depth, width), BF16),
            shape((rows, width), BF16),
        ],
        compiler_params=params(),
        cost_estimate=cost(rows * cols, 6 * width * width),
        name="start",
    )(where, token_mask, pair, token_mask, line(start_gain), start_in)

    swap = [(n, lax.axis_size("row") - 1 - n) for n in range(lax.axis_size("row"))]
    state_b = lax.ppermute(state, "row", swap)
    total_b = lax.ppermute(total, "row", swap)

    wide = 16
    broad = math.gcd(rows, 16)
    steps = rows // broad
    chunks = column_chunks(cols, slots)
    extra_slabs = [pl.cdiv(size // slots, depth) for _, size in chunks]
    rooms = [slots * depth * more for more in extra_slabs]
    slabs = [
        (slots // 2, size // slots + more, depth, width)
        for (_, size), more in zip(chunks, extra_slabs)
    ]

    column = lambda n: pl.BlockSpec(
        (width, width), lambda *_: (0, n), pipeline_mode=pl.Buffered(1)
    )

    def middle(part, update, gain):
        offset, chunk = chunks[part]
        span = chunk // 2
        low = lambda n: jnp.minimum(n, steps - 1)
        high = lambda n: jnp.maximum(n - steps, 0)
        tile = pl.BlockSpec((broad, chunk, width), lambda n, *_: (low(n), offset // chunk, 0))
        by_col = lambda *dims: pl.BlockSpec(dims, lambda n, *_: (high(n), 0, 0))
        extra = [] if update is None else [update]
        return pl.pallas_call(
            functools.partial(middle_kernel, steps, offset),
            grid_spec=pltpu.PrefetchScalarGridSpec(
                num_scalar_prefetch=2,
                grid=(steps + chunk // span,),
                in_specs=[
                    *[pl.BlockSpec(memory_space=pl.ANY)] * 5,
                    whole((rows, width)),
                    whole((rows, width)),
                    whole(token_mask.shape),
                    whole((1, width)),
                    whole((width, width)),
                    whole((1, width)),
                    column(1),
                    column(2),
                ]
                + [pl.BlockSpec(memory_space=pl.ANY)] * len(extra),
                out_specs=[
                    tile,
                    by_col(span, rows, width),
                    *[pl.BlockSpec(slabs[part], lambda *_: (0, 0, 0, 0))] * 2,
                ],
                scratch_shapes=[
                    pltpu.VMEM((rows * chunk, width), F32),
                    pltpu.VMEM((rooms[part], width), F32),
                    pltpu.VMEM((2 * width, width), BF16),
                    pltpu.VMEM((2, *slabs[part]), BF16),
                    *[pltpu.VMEM((rows, chunk, width), BF16)] * 3,
                    *[pltpu.VMEM((rows, depth, width), BF16)] * 2,
                    pltpu.SemaphoreType.DMA((steps, 5)),
                ],
            ),
            out_shape=[
                shape((rows, cols, width), BF16),
                shape((chunk, rows, width), BF16),
                *[shape(slabs[part], BF16)] * 2,
            ],
            input_output_aliases={15: 0} if extra else {},
            compiler_params=params(),
            cost_estimate=cost(rows * chunk, 7 * width * width),
            name="middle",
        )(
            where,
            token_mask,
            pair,
            query,
            gate,
            state,
            state_b,
            total,
            total_b,
            token_mask,
            line(start_head_gain),
            start_out,
            gain,
            end_in,
            end_in,
            *extra,
        )

    def queries(normed):
        chunk = normed.shape[0]
        span = chunk // 2
        return pl.pallas_call(
            query_kernel,
            grid=(chunk // span,),
            in_specs=[block(span, rows, width), column(0), column(3)],
            out_specs=[block(span, rows, width)] * 2,
            out_shape=[shape((chunk, rows, width), BF16)] * 2,
            compiler_params=params(),
            cost_estimate=cost(rows * chunk, 2 * width * width),
            name="queries",
        )(normed, end_in, end_in)

    def end(part, update_start, parts, outs, gain):
        offset, chunk = chunks[part]
        tile = pl.BlockSpec((rows, wide, width), lambda n, *_: (0, offset // wide + n, 0))
        return pl.pallas_call(
            end_kernel,
            grid_spec=pltpu.PrefetchScalarGridSpec(
                num_scalar_prefetch=1,
                grid=(chunk // wide,),
                in_specs=[
                    tile,
                    tile,
                    block(wide, rows, width),
                    block(wide, rows, width),
                    whole(slabs[part]),
                    whole(slabs[part]),
                    whole((1, width)),
                    whole((width, width)),
                    whole((1, width)),
                    whole((width, 2 * hidden)),
                    whole((hidden, width)),
                ]
                + [pl.BlockSpec(memory_space=pl.ANY)] * len(outs),
                out_specs=[tile, tile],
                scratch_shapes=[
                    pltpu.VMEM((rows * wide, width), F32),
                    pltpu.VMEM((rooms[part], width), F32),
                    pltpu.VMEM((2 * width, width), BF16),
                    pltpu.VMEM((2, *slabs[part]), BF16),
                ],
            ),
            out_shape=[shape((rows, cols, width), BF16)] * 2,
            input_output_aliases={12: 0, 13: 1} if outs else {},
            compiler_params=params(),
            cost_estimate=cost(rows * chunk, 2 * width * width + 3 * width * hidden),
            name="end",
        )(
            where,
            pair,
            update_start,
            *parts,
            line(end_head_gain),
            end_out,
            gain,
            trans_in,
            trans_out,
            *outs,
        )

    sums = []
    latest = []

    def advance(done):
        live = [n for n, (_, other) in enumerate(latest) if other is not None]
        if not live:
            return done, []
        done, *others = lax.optimization_barrier((done, *(latest[n][1] for n in live)))
        for n, other in zip(live, others):
            latest[n] = sums[n].send(other)
        return done, [*others, *jax.tree.leaves([latest[n][0] for n in live])]

    def after(value, behind):
        return lax.optimization_barrier((value, *behind))[0] if behind else value

    update_start = None
    outs = ()
    held = []
    behind = []
    for part in range(len(chunks)):
        update_start, normed, send, keep = middle(
            part, update_start, after(line(end_gain), behind)
        )
        held.append(normed)
        if part > 0 and part == len(chunks) - 1:
            held[0] = queries(after(held[0], [send]))
            first, behind = advance(held[0][0])
            held[0] = (first, held[0][1])
        else:
            send, behind = advance(send)
        sums.append(column_sum(send, keep))
        latest.append(next(sums[-1]))
        behind.append(latest[-1][0])
    waiting = list(range(1 if len(chunks) > 1 else 0, len(chunks)))
    for part in range(len(chunks)):
        while latest[part][1] is not None:
            batch = waiting
            waiting = waiting[len(batch) :]
            for n in batch:
                held[n] = queries(after(held[n], behind))
            if batch:
                first, behind = advance(held[batch[-1]][0])
                held[batch[-1]] = (first, held[batch[-1]][1])
            else:
                _, behind = advance(line(trans_gain))
        for n in waiting:
            held[n] = queries(held[n])
        waiting = []
        gain = after(line(trans_gain), behind)
        outs = end(part, update_start, (*held[part], *latest[part][0]), outs, gain)
        first, behind = advance(outs[0])
        outs = (first, outs[1])
    return (update_start, outs[0], outs[1])


def solution(mesh):
    pair_spec = P(("groups", "col"), "row", None)
    return jax.shard_map(
        shards,
        mesh=mesh,
        in_specs=(pair_spec, P("groups")) + (P(),) * 11,
        out_specs=(pair_spec,) * 3,
        check_vma=False,
    )
```
